128 devices in a mesh: dp: 128 (over y, z, x, core).
Axes of the slice: x: 4, y: 4, z: 4, core: 2. Of those that a mesh axis runs over, the one named last changes fastest.
Arguments:
- events: bfloat16 [131072, 512], P('dp'), may hold values from -6 to 6
- home_slot: int32 [131072], P('dp'), may hold values from 0 to 1024, as said below
- dest_slot: int32 [131072], P('dp'), may hold values from 0 to 1024, as said below
- seq_lens: int32 [256], P('dp'), may hold values from 0 to 1024, as said below
- weights: bfloat16 [512, 2560], replicated, may hold values from -0.25 to 0.25
- out_grad: bfloat16 [131072, 512], P('dp'), may hold values from -6 to 6
- momentum_in: float32 [512, 2048], P('dp'), may hold values from -3 to 3
- momentum_out: float32 [512, 512], P('dp'), may hold values from -3 to 3
Outputs:
- event_grad: bfloat16 [131072, 512], P('dp')
- new_momentum_in: float32 [512, 2048], P('dp')
- new_momentum_out: float32 [512, 512], P('dp')
The draws below stay inside these ranges and needn't reach their ends.
Inputs may be any that keep to these rules, and one draw needn't show every extreme that they name: `seq_lens`: each device's 2 entries are the lengths of the sequences placed on it, in order, then zeros; the sequences' blocks, ceil(length / 512) each, add up to at most 2. `dest_slot`: for each row of a device's blocks: 1024 if the row lies in no sequence, else s * 8 + k, where s is the device that holds the row's event at home and k its slot among the rows that s sends to this device; no value below 1024 repeats on a device. `home_slot`: for each home row: 1024 if no sequence uses it, else t * 8 + k, where t is the device that takes the row and k its slot as in dest_slot; no value below 1024 repeats on a device, and the two arrays name the same rows. A device sends at most 8 rows to one device, and in every draw some device receives 8 rows from every device.
All inputs are finite; a program needn't handle non-finite values.
Results may differ from the reference program's by a relative error of at most 0.0085.
Values may be sent and summed in bfloat16 or wider, within the bound.
No kernel may reach another device: no remote copies, remote signals or barrier semaphores. Data moves between devices by JAX's collectives and lax.ppermute only.
A program may use at most 128 MiB of HBM per device.

```python
import jax
import jax.numpy as jnp
from jax import lax

D = 512
HEADS = 8
BLK = 512
NBLK = 2
DEV_ROWS = 1024
ROWS = 131072


def row_owner_drawn(lengths, row_count):
    blocks = (lengths + BLK - 1) // BLK
    starts = (jnp.cumsum(blocks) - blocks) * BLK
    places = jnp.arange(row_count, dtype=jnp.int32)
    inside = (places[:, None] >= starts[None, :]) & (places[:, None] < starts[None, :] + lengths[None, :])
    labels = jnp.arange(lengths.shape[0], dtype=jnp.int32) + 1
    return (jnp.sum(jnp.where(inside, labels[None, :], 0), axis=1) - 1).astype(jnp.int32)


def placement_plan(base_key):
    devices = ROWS // DEV_ROWS
    capacity = DEV_ROWS // devices
    subkeys = jax.random.split(jax.random.fold_in(base_key, 7177), 6)
    device_ids = jnp.arange(devices, dtype=jnp.int32)
    block_ids = jnp.arange(NBLK, dtype=jnp.int32)
    used_blocks = jax.random.randint(subkeys[0], (devices,), (NBLK + 1) // 2, NBLK + 1, dtype=jnp.int32)
    crowded = jax.random.randint(subkeys[1], (), 0, devices, dtype=jnp.int32)
    used_blocks = jnp.where(device_ids == crowded, NBLK, used_blocks)
    breaks = jax.random.randint(subkeys[2], (devices, NBLK), 0, 2, dtype=jnp.int32)
    in_use = block_ids[None, :] < used_blocks[:, None]
    begins = jnp.where(block_ids[None, :] == 0, 1, breaks) * in_use.astype(jnp.int32)
    sequence_ids = (jnp.cumsum(begins, axis=1) - 1).astype(jnp.int32)
    matches = (sequence_ids[:, :, None] == block_ids[None, None, :]) & in_use[:, :, None]
    counts = jnp.sum(matches.astype(jnp.int32), axis=1).astype(jnp.int32)
    tail_rows = jax.random.randint(subkeys[3], (devices, NBLK), 1, BLK + 1, dtype=jnp.int32)
    tail_rows = jnp.where((device_ids == crowded)[:, None], BLK, tail_rows)
    lengths = jnp.where(counts > 0, (counts - 1) * BLK + tail_rows, 0).astype(jnp.int32)
    owners = jax.vmap(lambda entry: row_owner_drawn(entry, DEV_ROWS))(lengths)
    live_rows = (owners >= 0).astype(jnp.int32)
    rank_order = (jnp.cumsum(live_rows, axis=1) - 1).astype(jnp.int32)
    groups = jnp.clip(rank_order // capacity, 0, devices - 1)
    within = rank_order % capacity
    offsets = jax.random.permutation(subkeys[4], devices).astype(jnp.int32)
    sources = (device_ids[:, None] + offsets[groups]) % devices
    dest_slot = jnp.where(live_rows > 0, sources * capacity + within, DEV_ROWS).astype(jnp.int32)
    totals = jnp.sum(live_rows, axis=1).astype(jnp.int32)
    places = jnp.arange(DEV_ROWS, dtype=jnp.int32)
    place_group = places // capacity
    place_within = places % capacity
    targets = (device_ids[:, None] - offsets[place_group][None, :]) % devices
    values = jnp.where(places[None, :] < totals[targets], targets * capacity + place_within[None, :], DEV_ROWS).astype(jnp.int32)
    orders = jax.vmap(lambda subkey: jax.random.permutation(subkey, DEV_ROWS))(jax.random.split(subkeys[5], devices)).astype(jnp.int32)
    home_slot = jnp.zeros((devices, DEV_ROWS), jnp.int32).at[device_ids[:, None], orders].set(values)
    return (lengths, home_slot, dest_slot)


def draw_seq_lens(key, part):
    return placement_plan(key)[0].reshape(-1)


def draw_home_slot(key, part):
    return placement_plan(key)[1].reshape(-1)


def draw_dest_slot(key, part):
    return placement_plan(key)[2].reshape(-1)


def steps_of(rng, extent, cuts, smallest, largest):
    def one(dim, shards_of):
        steps = jax.random.uniform(jax.random.fold_in(jax.random.fold_in(rng, 6), dim), (shards_of,), jnp.float32, smallest / len(cuts), largest / len(cuts))
        return jnp.repeat(jnp.exp(steps), extent[dim] // shards_of).reshape((-1,) + (1,) * (len(extent) - dim - 1))

    level = one(*cuts[0])
    for cut in cuts[1:]:
        level = level * one(*cut)
    return level


def bell_draw(stream_key, dims, scale, most, cuts=(), kind=jnp.bfloat16):
    array = jax.random.normal(stream_key, dims, jnp.float32) * scale
    if len(cuts) > 0:
        array = steps_of(stream_key, dims, cuts, -0.22, 0.18) * array
    return jnp.clip(array, min=-most, max=most).astype(kind)


def setup_inputs(seed: int = 0) -> dict:
    streams_of = jax.random.split(jax.random.key(seed), 9)
    events = bell_draw(streams_of[0], (ROWS, D), 1.0, 6.0, ((0, 128),))
    home_slot = draw_home_slot(jax.random.fold_in(streams_of[8], 71), 0)
    dest_slot = draw_dest_slot(jax.random.fold_in(streams_of[8], 71), 0)
    seq_lens = draw_seq_lens(jax.random.fold_in(streams_of[8], 71), 0)
    weights = bell_draw(streams_of[4], (D, 5 * D), D ** -0.5, 0.25)
    out_grad = bell_draw(streams_of[5], (ROWS, D), 1.0, 6.0, ((0, 128),))
    momentum_in = bell_draw(streams_of[6], (D, 4 * D), 0.5, 3.0, ((0, 128),), jnp.float32)
    momentum_out = bell_draw(streams_of[7], (D, D), 0.5, 3.0, ((0, 128),), jnp.float32)
    return {"events": events, "home_slot": home_slot, "dest_slot": dest_slot, "seq_lens": seq_lens, "weights": weights, "out_grad": out_grad, "momentum_in": momentum_in, "momentum_out": momentum_out}


NORM_EPS = 1e-05
DECAY = 0.9

def row_owner(lengths, row_count):
    blocks = (lengths + BLK - 1) // BLK
    starts = (jnp.cumsum(blocks) - blocks) * BLK
    places = jnp.arange(row_count, dtype=jnp.int32)
    inside = (places[:, None] >= starts[None, :]) & (places[:, None] < starts[None, :] + lengths[None, :])
    labels = jnp.arange(lengths.shape[0], dtype=jnp.int32) + 1
    return (lax.optimization_barrier(jnp.sum(jnp.where(inside, labels[None, :], 0), axis=1)) - 1).astype(jnp.int32)

def attend_pair(queries, key_rows, value_rows, query_owner, key_owner, query_place, key_place):
    factor = queries.shape[2] ** (-0.5)
    scores = jnp.einsum('qhe,khe->hqk', queries.astype(jnp.float32), key_rows.astype(jnp.float32)) * factor
    allowed = (query_owner[:, None] == key_owner[None, :]) & (query_owner[:, None] >= 0) & (key_place[None, :] <= query_place[:, None])
    weights = jnp.where(allowed[None], jax.nn.silu(scores), 0.0).astype(jnp.bfloat16)
    return jnp.einsum('hqk,khe->qhe', weights.astype(jnp.float32), value_rows.astype(jnp.float32))

def mixing(hidden, owners):
    activated = jax.nn.silu(hidden)
    model_width = hidden.shape[1] // 4
    row_count = hidden.shape[0]
    head_size = model_width // HEADS
    gate_part = activated[:, :model_width]
    value_set = activated[:, model_width:2 * model_width].astype(jnp.bfloat16).reshape(row_count, HEADS, head_size)
    query_set = activated[:, 2 * model_width:3 * model_width].astype(jnp.bfloat16).reshape(row_count, HEADS, head_size)
    key_set = activated[:, 3 * model_width:].astype(jnp.bfloat16).reshape(row_count, HEADS, head_size)
    places = jnp.arange(row_count, dtype=jnp.int32)
    pieces = []
    for qblock in range(row_count // BLK):
        low_row = qblock * BLK
        high_row = low_row + BLK
        pieces.append(jax.checkpoint(attend_pair)(query_set[low_row:high_row], key_set[:high_row], value_set[:high_row], owners[low_row:high_row], owners[:high_row], places[low_row:high_row], places[:high_row]))
    attended = jnp.concatenate(pieces, axis=0).reshape(row_count, model_width)
    centre = lax.optimization_barrier(jnp.mean(attended, axis=1, keepdims=True))
    centred = attended - centre
    spread = lax.optimization_barrier(jnp.mean(centred * centred, axis=1, keepdims=True))
    return centred * lax.rsqrt(spread + NORM_EPS) * gate_part

def device_grads(tokens, upstream, weights, lengths):
    model_width = tokens.shape[1]
    owners = row_owner(lengths, tokens.shape[0])
    w_in = weights[:, :4 * model_width]
    w_out = weights[:, 4 * model_width:]
    hidden = jnp.dot(tokens, w_in, preferred_element_type=jnp.float32)
    mixed_out, pullback = jax.vjp(lambda hidden_in: mixing(hidden_in, owners), hidden)
    mixed_low = mixed_out.astype(jnp.bfloat16)
    mixed_grad = jnp.dot(upstream, w_out.T, preferred_element_type=jnp.float32)
    hidden_grad = pullback(mixed_grad)[0].astype(jnp.bfloat16)
    token_grad = (upstream.astype(jnp.float32) + jnp.dot(hidden_grad, w_in.T, preferred_element_type=jnp.float32)).astype(jnp.bfloat16)
    in_term = jnp.dot(tokens.T, hidden_grad, preferred_element_type=jnp.float32)
    out_term = jnp.dot(mixed_low.T, upstream, preferred_element_type=jnp.float32)
    return (token_grad, in_term, out_term)

def reference(events, home_slot, dest_slot, seq_lens, weights, out_grad, momentum_in, momentum_out):
    devices = ROWS // DEV_ROWS
    capacity = DEV_ROWS // devices
    model_width = events.shape[1]
    row_ids = jnp.arange(ROWS, dtype=jnp.int32)
    device_of = (row_ids // DEV_ROWS).astype(jnp.int32)
    send_keys = jnp.where(home_slot < DEV_ROWS, device_of * DEV_ROWS + home_slot, ROWS).astype(jnp.int32)
    lookup_table = jnp.full((ROWS + 1,), ROWS, dtype=jnp.int32).at[send_keys].set(row_ids)
    lookup_table = jnp.concatenate([lookup_table[:ROWS], jnp.full((1,), ROWS, dtype=jnp.int32)])
    receive_keys = jnp.where(dest_slot < DEV_ROWS, dest_slot // capacity * DEV_ROWS + device_of * capacity + dest_slot % capacity, ROWS).astype(jnp.int32)
    sources = lookup_table[receive_keys]
    padded = jnp.concatenate([events, jnp.zeros((1, model_width), jnp.bfloat16)], axis=0)
    tokens = padded[sources]

    def visit_device(running, entries):
        token_grad, in_term, out_term = device_grads(entries[0], entries[1], weights, entries[2])
        return ((running[0] + in_term, running[1] + out_term), token_grad)
    initial = (jnp.zeros((model_width, 4 * model_width), jnp.float32), jnp.zeros((model_width, model_width), jnp.float32))
    sums, token_grads = lax.scan(visit_device, initial, (tokens.reshape(devices, DEV_ROWS, model_width), out_grad.reshape(devices, DEV_ROWS, model_width), seq_lens.reshape(devices, NBLK)))
    event_grad = jnp.zeros((ROWS + 1, model_width), jnp.bfloat16).at[sources].set(token_grads.reshape(ROWS, model_width))[:ROWS]
    grad_scale = ROWS ** (-0.5)
    return (event_grad, DECAY * momentum_in + grad_scale * sums[0], DECAY * momentum_out + grad_scale * sums[1])
```

```python
import functools

import jax
import jax.numpy as jnp
from jax import lax
from jax.experimental import pallas as pl
from jax.experimental.pallas import tpu as pltpu
from jax.sharding import Mesh
from jax.sharding import PartitionSpec as P

BLK = 512
DP = ("dp_0", "dp_1", "dp_2", "dp_3")
CHIPS = DP[:3]
CORE = DP[3]

NORM_EPS = 1e-05
DECAY = 0.9
TILE = 256
BF = jnp.bfloat16
F32 = jnp.float32


def dot(a, b):
    return jnp.dot(a, b, preferred_element_type=F32)


def dot_nt(a, b):
    return lax.dot_general(a, b, (((1,), (1,)), ((), ())), preferred_element_type=F32)


def dot_tn(a, b):
    return lax.dot_general(a, b, (((0,), (0,)), ((), ())), preferred_element_type=F32)


def rows_at(i):
    return pl.ds(pl.multiple_of(i * TILE, TILE), TILE)


def slot_rows(slots, first, count):
    places = lax.broadcasted_iota(jnp.int32, (count, slots.shape[1]), 0) + first
    return jnp.where(slots == places, 1.0, 0.0).astype(BF)


def slot_columns(spread, count):
    lane = lax.broadcasted_iota(jnp.int32, spread.shape, 1)
    parts = [
        jnp.where(spread == lane + at, 1.0, 0.0).astype(BF) for at in range(0, count, 128)
    ]
    return jnp.concatenate(parts, axis=1)


def spread_slots(slots):
    return jnp.transpose(jnp.broadcast_to(slots, (128, slots.shape[1])))


def place_kernel(slots_ref, rows_ref, out_ref):
    @pl.loop(0, out_ref.shape[0] // TILE)
    def _(i):
        pick = slot_rows(slots_ref[...], i * TILE, TILE)
        out_ref[rows_at(i), :] = dot(pick, rows_ref[...]).astype(BF)


def fetch_kernel(slots_ref, rows_ref, out_ref, spread_ref):
    spread_ref[...] = spread_slots(slots_ref[...])

    @pl.loop(0, out_ref.shape[0] // TILE)
    def _(i):
        pick = slot_columns(spread_ref[rows_at(i), :], rows_ref.shape[0])
        out_ref[rows_at(i), :] = dot(pick, rows_ref[...]).astype(BF)


def silu_parts(half):
    plus = 1.0 + jnp.tanh(half)
    value = half * plus
    return value, plus + value * (2.0 - plus)


def two_heads(rows):
    lane = lax.broadcasted_iota(jnp.int32, rows.shape, 1)
    none = jnp.zeros_like(rows)
    low = lane < 64
    return jnp.concatenate([jnp.where(low, rows, none), jnp.where(low, none, rows)], axis=0)


def own_lanes(stacked):
    half = stacked.shape[0] // 2
    lane = lax.broadcasted_iota(jnp.int32, (half, stacked.shape[1]), 1)
    return jnp.where(lane < 64, stacked[:half], stacked[half:])


def layer_kernel(
    lens_ref,
    dest_ref,
    inbox_ref,
    weights_ref,
    upstream_ref,
    sendback_ref,
    grads_ref,
    spread_ref,
    tokens_t,
    slope,
    gate,
    vals,
    queries,
    keys,
    attended,
    mixed_t,
    att_grad,
    near_w,
    near_d,
    far_w,
    far_d,
    key_sum,
    val_sum,
    hidden_grad,
    token_grad,
):
    row_count, width = inbox_ref.shape
    tiles = row_count // TILE
    pairs = width // 128
    first, second = lens_ref[0], lens_ref[1]
    joined = jnp.where(first > 0, first, second) > BLK
    spread_ref[...] = spread_slots(dest_ref[...])

    @pl.loop(0, tiles)
    def _(i):
        rows = rows_at(i)
        pick = slot_columns(spread_ref[rows, :], row_count)
        tokens = dot(pick, inbox_ref[...]).astype(BF)
        tokens_t[:, rows] = tokens.T
        for g in range(4):
            columns = slice(g * width, (g + 1) * width)
            half = dot(tokens, weights_ref[:, columns]) * 0.5
            value, slope2 = silu_parts(half)
            slope[rows, columns] = 0.5 * slope2
            if g == 0:
                gate[rows, :] = value
            elif g == 1:
                vals[rows, :] = value.astype(BF)
            elif g == 2:
                queries[rows, :] = value.astype(BF) * jnp.asarray(0.0625, BF)
            else:
                keys[rows, :] = value.astype(BF)

    @pl.loop(0, pairs)
    def _(p):
        lanes = pl.ds(pl.multiple_of(p * 128, 128), 128)
        for i in range(tiles):
            rows = slice(i * TILE, (i + 1) * TILE)
            stacked = two_heads(queries[rows, lanes])
            low, high = (i * TILE) // BLK * BLK, (i + 1) * TILE
            span = high - low
            weight, slope2 = silu_parts(dot_nt(stacked, keys[low:high, lanes]))
            place = lax.broadcasted_iota(jnp.int32, (TILE, span), 0) + (i * TILE - low)
            seen = lax.broadcasted_iota(jnp.int32, (TILE, span), 1) <= place
            seen = jnp.concatenate([seen, seen], axis=0)
            weight = jnp.where(seen, weight, 0.0).astype(BF)
            near_w[p, i, :, :span] = weight
            near_d[p, i, :, :span] = jnp.where(seen, slope2, 0.0).astype(BF)
            attended[rows, lanes] = own_lanes(dot(weight, vals[low:high, lanes]))
            if low > 0:

                @pl.when(joined)
                def _(i=i, rows=rows, stacked=stacked, low=low):
                    weight, slope2 = silu_parts(dot_nt(stacked, keys[:low, lanes]))
                    weight = weight.astype(BF)
                    j = i - low // TILE
                    far_w[p, j] = weight
                    far_d[p, j] = slope2.astype(BF)
                    attended[rows, lanes] += own_lanes(dot(weight, vals[:low, lanes]))

    @pl.loop(0, tiles)
    def _(i):
        rows = rows_at(i)
        value = attended[rows, :]
        centre = jnp.mean(value, axis=1, keepdims=True)
        centred = value - centre
        spread = jnp.mean(centred * centred, axis=1, keepdims=True)
        scale = lax.rsqrt(spread + NORM_EPS)
        normed = centred * scale
        gates = gate[rows, :]
        mixed_t[:, rows] = (normed * gates).astype(BF).T
        mixed_grad = dot_nt(upstream_ref[rows, :], weights_ref[:, 4 * width :])
        hidden_grad[rows, :width] = (mixed_grad * normed * slope[rows, :width]).astype(BF)
        down = mixed_grad * gates
        mean_down = jnp.mean(down, axis=1, keepdims=True)
        mean_both = jnp.mean(down * normed, axis=1, keepdims=True)
        att_grad[rows, :] = (scale * (down - mean_down - normed * mean_both)).astype(BF)

    @pl.loop(0, pairs)
    def _(p):
        start = pl.multiple_of(p * 128, 128)
        lanes = pl.ds(start, 128)
        key_sum[...] = jnp.zeros_like(key_sum)
        val_sum[...] = jnp.zeros_like(val_sum)
        query_lanes = pl.ds(pl.multiple_of(start + 2 * width, 128), 128)
        for i in range(tiles):
            rows = slice(i * TILE, (i + 1) * TILE)
            stacked = two_heads(queries[rows, lanes])
            down = two_heads(att_grad[rows, lanes])
            low, high = (i * TILE) // BLK * BLK, (i + 1) * TILE
            span = high - low
            score = dot_nt(down, vals[low:high, lanes]).astype(BF) * near_d[p, i, :, :span]
            val_sum[low:high] += dot_tn(near_w[p, i, :, :span], down)
            key_sum[low:high] += dot_tn(score, stacked)
            attended[rows, :128] = own_lanes(dot(score, keys[low:high, lanes]))
            if low > 0:

                @pl.when(joined)
                def _(i=i, rows=rows, stacked=stacked, down=down, low=low):
                    j = i - low // TILE
                    score = dot_nt(down, vals[:low, lanes]).astype(BF) * far_d[p, j]
                    val_sum[:low] += dot_tn(far_w[p, j], down)
                    key_sum[:low] += dot_tn(score, stacked)
                    attended[rows, :128] += own_lanes(dot(score, keys[:low, lanes]))

        for source, group, factor in ((val_sum, 1, 1.0), (attended, 2, 0.0625), (key_sum, 3, 1.0)):
            columns = pl.ds(pl.multiple_of(start + group * width, 128), 128)
            rounded = (source[:, :128] * factor).astype(BF).astype(F32)
            hidden_grad[:, columns] = (rounded * slope[:, columns]).astype(BF)

    @pl.loop(0, tiles)
    def _(i):
        rows = rows_at(i)
        total = dot_nt(hidden_grad[rows, :], weights_ref[:, : 4 * width])
        token_grad[rows, :] = (upstream_ref[rows, :].astype(F32) + total).astype(BF)

    @pl.loop(0, tiles)
    def _(i):
        pick = slot_rows(dest_ref[...], i * TILE, TILE)
        sendback_ref[rows_at(i), :] = dot(pick, token_grad[...]).astype(BF)

    @pl.loop(0, 4 * width // TILE)
    def _(i):
        columns = rows_at(i)
        grads_ref[:, columns] = dot(tokens_t[...], hidden_grad[:, columns]).astype(BF)

    grads_ref[:, 4 * width :] = dot(mixed_t[...], upstream_ref[...]).astype(BF)


VMEM_SPEC = pl.BlockSpec(memory_space=pltpu.VMEM)
SMEM_SPEC = pl.BlockSpec(memory_space=pltpu.SMEM)


def place(slots, rows):
    count, width = rows.shape
    return pl.pallas_call(
        place_kernel,
        name="place_rows",
        out_shape=jax.ShapeDtypeStruct((count, width), BF),
        in_specs=[VMEM_SPEC] * 2,
        out_specs=VMEM_SPEC,
        cost_estimate=pl.CostEstimate(
            flops=2 * count * count * width, bytes_accessed=4 * count * width, transcendentals=0
        ),
    )(slots, rows)


def fetch(slots, rows):
    count, width = rows.shape
    return pl.pallas_call(
        fetch_kernel,
        name="fetch_rows",
        out_shape=jax.ShapeDtypeStruct((count, width), BF),
        in_specs=[VMEM_SPEC] * 2,
        out_specs=VMEM_SPEC,
        scratch_shapes=[pltpu.VMEM((count, 128), jnp.int32)],
        cost_estimate=pl.CostEstimate(
            flops=2 * count * count * width, bytes_accessed=4 * count * width, transcendentals=0
        ),
    )(slots, rows)


def layer(lens, dest, inbox, weights, upstream):
    count, width = inbox.shape
    tiles, pairs, far = count // TILE, width // 128, (count - BLK) // TILE
    return pl.pallas_call(
        layer_kernel,
        name="layer_step",
        out_shape=(
            jax.ShapeDtypeStruct((count, width), BF),
            jax.ShapeDtypeStruct(weights.shape, BF),
        ),
        in_specs=[SMEM_SPEC] + [VMEM_SPEC] * 4,
        out_specs=(VMEM_SPEC, VMEM_SPEC),
        scratch_shapes=[
            pltpu.VMEM((count, 128), jnp.int32),
            pltpu.VMEM((width, count), BF),
            pltpu.VMEM((count, 4 * width), F32),
            pltpu.VMEM((count, width), F32),
            pltpu.VMEM((count, width), BF),
            pltpu.VMEM((count, width), BF),
            pltpu.VMEM((count, width), BF),
            pltpu.VMEM((count, width), F32),
            pltpu.VMEM((width, count), BF),
            pltpu.VMEM((count, width), BF),
            pltpu.VMEM((pairs, tiles, 2 * TILE, BLK), BF),
            pltpu.VMEM((pairs, tiles, 2 * TILE, BLK), BF),
            pltpu.VMEM((pairs, far, 2 * TILE, BLK), BF),
            pltpu.VMEM((pairs, far, 2 * TILE, BLK), BF),
            pltpu.VMEM((count, 128), F32),
            pltpu.VMEM((count, 128), F32),
            pltpu.VMEM((count, 4 * width), BF),
            pltpu.VMEM((count, width), BF),
        ],
        compiler_params=pltpu.CompilerParams(vmem_limit_bytes=60 << 20),
        cost_estimate=pl.CostEstimate(
            flops=30_000_000_000, bytes_accessed=12_000_000, transcendentals=10_000_000
        ),
    )(lens, dest, inbox, weights, upstream)


def core_swap(value):
    return lax.ppermute(value, CORE, [(0, 1), (1, 0)])


def summed_rows(grads):
    rows, columns = grads.shape
    chips = lax.axis_size(CHIPS)
    half = columns // 2
    core = lax.axis_index(CORE)
    mine = lax.dynamic_slice_in_dim(grads, core * half, half, axis=1)
    other = lax.dynamic_slice_in_dim(grads, (1 - core) * half, half, axis=1)
    both = (mine.astype(F32) + core_swap(other).astype(F32)).astype(BF)
    spread = both.reshape(chips, rows // chips, half)
    arrived = lax.all_to_all(spread, CHIPS, split_axis=0, concat_axis=0, tiled=True)
    total = arrived.astype(F32).sum(axis=0)
    keep = rows // chips // 2
    mine = lax.dynamic_slice_in_dim(total, core * keep, keep, axis=0)
    other = core_swap(lax.dynamic_slice_in_dim(total, (1 - core) * keep, keep, axis=0))
    return jnp.where(
        core == 0,
        jnp.concatenate([mine, other], axis=1),
        jnp.concatenate([other, mine], axis=1),
    )


def shards(events, home_slot, dest_slot, seq_lens, weights, out_grad, momentum_in, momentum_out):
    row_count, model_width = events.shape
    home = home_slot.reshape(1, row_count)
    dest = dest_slot.reshape(1, row_count)
    peers = lax.axis_size(DP)

    def exchange(rows):
        blocks = rows.reshape(peers, row_count // peers, model_width)
        arrived = lax.all_to_all(blocks, DP, split_axis=0, concat_axis=0, tiled=True)
        return arrived.reshape(row_count, model_width)

    inbox = exchange(place(home, events))
    sendback, grads = layer(seq_lens, dest, inbox, weights, out_grad)
    event_grad = fetch(home, exchange(sendback))
    total = summed_rows(grads)
    grad_scale = (peers * row_count) ** (-0.5)
    return (
        event_grad,
        DECAY * momentum_in + grad_scale * total[:, : 4 * model_width],
        DECAY * momentum_out + grad_scale * total[:, 4 * model_width :],
    )


def solution(mesh):
    split = Mesh(mesh.devices.reshape(4, 4, 4, 2), DP)
    return jax.shard_map(
        shards,
        mesh=split,
        in_specs=(P(DP, None), P(DP), P(DP), P(DP), P(), P(DP, None), P(DP, None), P(DP, None)),
        out_specs=(P(DP, None), P(DP, None), P(DP, None)),
        check_vma=False,
    )
```

```python
import functools

import jax
import jax.numpy as jnp
from jax import lax
from jax.experimental import pallas as pl
from jax.experimental.pallas import tpu as pltpu
from jax.sharding import Mesh
from jax.sharding import PartitionSpec as P

BLK = 512
DP = ("dp_0", "dp_1", "dp_2", "dp_3")
CHIPS = DP[:3]
CORE = DP[3]

NORM_EPS = 1e-05
DECAY = 0.9
TILE = 256
BF = jnp.bfloat16
F32 = jnp.float32


def dot(a, b):
    return jnp.dot(a, b, preferred_element_type=F32)


def dot_nt(a, b):
    return lax.dot_general(a, b, (((1,), (1,)), ((), ())), preferred_element_type=F32)


def dot_tn(a, b):
    return lax.dot_general(a, b, (((0,), (0,)), ((), ())), preferred_element_type=F32)


def rows_at(i):
    return pl.ds(pl.multiple_of(i * TILE, TILE), TILE)


def slot_rows(slots, first, count):
    places = lax.broadcasted_iota(jnp.int32, (count, slots.shape[1]), 0) + first
    return jnp.where(slots == places, 1.0, 0.0).astype(BF)


def slot_columns(spread, count):
    lane = lax.broadcasted_iota(jnp.int32, spread.shape, 1)
    parts = [
        jnp.where(spread == lane + at, 1.0, 0.0).astype(BF) for at in range(0, count, 128)
    ]
    return jnp.concatenate(parts, axis=1)


def spread_slots(slots):
    return jnp.transpose(jnp.broadcast_to(slots, (128, slots.shape[1])))


def place_kernel(slots_ref, rows_ref, out_ref):
    @pl.loop(0, out_ref.shape[0] // TILE)
    def _(i):
        pick = slot_rows(slots_ref[...], i * TILE, TILE)
        out_ref[rows_at(i), :] = dot(pick, rows_ref[...]).astype(BF)


def silu_parts(half):
    plus = 1.0 + jnp.tanh(half)
    value = half * plus
    return value, plus + value * (2.0 - plus)


def two_heads(rows):
    lane = lax.broadcasted_iota(jnp.int32, rows.shape, 1)
    none = jnp.zeros_like(rows)
    low = lane < 64
    return jnp.concatenate([jnp.where(low, rows, none), jnp.where(low, none, rows)], axis=0)


def own_lanes(stacked):
    half = stacked.shape[0] // 2
    lane = lax.broadcasted_iota(jnp.int32, (half, stacked.shape[1]), 1)
    return jnp.where(lane < 64, stacked[:half], stacked[half:])


def layer_kernel(
    lens_ref,
    dest_ref,
    inbox_ref,
    weights_ref,
    upstream_ref,
    sendback_ref,
    kept_ref,
    given_ref,
    spread_ref,
    tokens_t,
    slope,
    gate,
    vals,
    queries,
    keys,
    attended,
    mixed_t,
    att_grad,
    near_w,
    near_d,
    far_w,
    far_d,
    key_sum,
    val_sum,
    hidden_grad,
    token_grad,
):
    row_count, width = inbox_ref.shape
    tiles = row_count // TILE
    pairs = width // 128
    first, second = lens_ref[0], lens_ref[1]
    joined = jnp.where(first > 0, first, second) > BLK
    spread_ref[...] = spread_slots(dest_ref[...])

    @pl.loop(0, tiles)
    def _(i):
        rows = rows_at(i)
        pick = slot_columns(spread_ref[rows, :], row_count)
        tokens = dot(pick, inbox_ref[...]).astype(BF)
        tokens_t[:, rows] = tokens.T
        for g in range(4):
            columns = slice(g * width, (g + 1) * width)
            half = dot(tokens, weights_ref[:, columns]) * 0.5
            value, slope2 = silu_parts(half)
            slope[rows, columns] = 0.5 * slope2
            if g == 0:
                gate[rows, :] = value
            elif g == 1:
                vals[rows, :] = value.astype(BF)
            elif g == 2:
                queries[rows, :] = value.astype(BF) * jnp.asarray(0.0625, BF)
            else:
                keys[rows, :] = value.astype(BF)

    @pl.loop(0, pairs)
    def _(p):
        lanes = pl.ds(pl.multiple_of(p * 128, 128), 128)
        for i in range(tiles):
            rows = slice(i * TILE, (i + 1) * TILE)
            stacked = two_heads(queries[rows, lanes])
            low, high = (i * TILE) // BLK * BLK, (i + 1) * TILE
            span = high - low
            weight, slope2 = silu_parts(dot_nt(stacked, keys[low:high, lanes]))
            place = lax.broadcasted_iota(jnp.int32, (TILE, span), 0) + (i * TILE - low)
            seen = lax.broadcasted_iota(jnp.int32, (TILE, span), 1) <= place
            seen = jnp.concatenate([seen, seen], axis=0)
            weight = jnp.where(seen, weight, 0.0).astype(BF)
            near_w[p, i, :, :span] = weight
            near_d[p, i, :, :span] = jnp.where(seen, slope2, 0.0).astype(BF)
            attended[rows, lanes] = own_lanes(dot(weight, vals[low:high, lanes]))
            if low > 0:

                @pl.when(joined)
                def _(i=i, rows=rows, stacked=stacked, low=low):
                    weight, slope2 = silu_parts(dot_nt(stacked, keys[:low, lanes]))
                    weight = weight.astype(BF)
                    j = i - low // TILE
                    far_w[p, j] = weight
                    far_d[p, j] = slope2.astype(BF)
                    attended[rows, lanes] += own_lanes(dot(weight, vals[:low, lanes]))

    @pl.loop(0, tiles)
    def _(i):
        rows = rows_at(i)
        value = attended[rows, :]
        centre = jnp.mean(value, axis=1, keepdims=True)
        centred = value - centre
        spread = jnp.mean(centred * centred, axis=1, keepdims=True)
        scale = lax.rsqrt(spread + NORM_EPS)
        normed = centred * scale
        gates = gate[rows, :]
        mixed_t[:, rows] = (normed * gates).astype(BF).T
        mixed_grad = dot_nt(upstream_ref[rows, :], weights_ref[:, 4 * width :])
        hidden_grad[rows, :width] = (mixed_grad * normed * slope[rows, :width]).astype(BF)
        down = mixed_grad * gates
        mean_down = jnp.mean(down, axis=1, keepdims=True)
        mean_both = jnp.mean(down * normed, axis=1, keepdims=True)
        att_grad[rows, :] = (scale * (down - mean_down - normed * mean_both)).astype(BF)

    @pl.loop(0, pairs)
    def _(p):
        start = pl.multiple_of(p * 128, 128)
        lanes = pl.ds(start, 128)
        key_sum[...] = jnp.zeros_like(key_sum)
        val_sum[...] = jnp.zeros_like(val_sum)
        query_lanes = pl.ds(pl.multiple_of(start + 2 * width, 128), 128)
        for i in range(tiles):
            rows = slice(i * TILE, (i + 1) * TILE)
            stacked = two_heads(queries[rows, lanes])
            down = two_heads(att_grad[rows, lanes])
            low, high = (i * TILE) // BLK * BLK, (i + 1) * TILE
            span = high - low
            score = dot_nt(down, vals[low:high, lanes]).astype(BF) * near_d[p, i, :, :span]
            val_sum[low:high] += dot_tn(near_w[p, i, :, :span], down)
            key_sum[low:high] += dot_tn(score, stacked)
            attended[rows, :128] = own_lanes(dot(score, keys[low:high, lanes]))
            if low > 0:

                @pl.when(joined)
                def _(i=i, rows=rows, stacked=stacked, down=down, low=low):
                    j = i - low // TILE
                    score = dot_nt(down, vals[:low, lanes]).astype(BF) * far_d[p, j]
                    val_sum[:low] += dot_tn(far_w[p, j], down)
                    key_sum[:low] += dot_tn(score, stacked)
                    attended[rows, :128] += own_lanes(dot(score, keys[:low, lanes]))

        for source, group, factor in ((val_sum, 1, 1.0), (attended, 2, 0.0625), (key_sum, 3, 1.0)):
            columns = pl.ds(pl.multiple_of(start + group * width, 128), 128)
            rounded = (source[:, :128] * factor).astype(BF).astype(F32)
            hidden_grad[:, columns] = (rounded * slope[:, columns]).astype(BF)

    @pl.loop(0, tiles)
    def _(i):
        rows = rows_at(i)
        total = dot_nt(hidden_grad[rows, :], weights_ref[:, : 4 * width])
        token_grad[rows, :] = (upstream_ref[rows, :].astype(F32) + total).astype(BF)

    @pl.loop(0, tiles)
    def _(i):
        pick = slot_rows(dest_ref[...], i * TILE, TILE)
        sendback_ref[rows_at(i), :] = dot(pick, token_grad[...]).astype(BF)

    halves = kept_ref.shape[1] // TILE
    ours = lax.axis_index(CORE)

    def put(value, i):
        half = i // halves
        columns = rows_at(i - half * halves)

        @pl.when(half == ours)
        def _():
            kept_ref[:, columns] = value

        @pl.when(half != ours)
        def _():
            given_ref[:, columns] = value

    inner = 4 * width // TILE

    @pl.loop(0, inner)
    def _(i):
        put(dot(tokens_t[...], hidden_grad[:, rows_at(i)]).astype(BF), i)

    for i in range(width // TILE):
        columns = slice(i * TILE, (i + 1) * TILE)
        put(dot(mixed_t[...], upstream_ref[:, columns]).astype(BF), inner + i)


def pack_kernel(rows_ref, kept_ref, got_ref, out_ref):
    peers, slots, width = rows_ref.shape
    half = kept_ref.shape[1] // 2
    out_ref[:, :, :width] = rows_ref[...]
    both = (kept_ref[...].astype(F32) + got_ref[...].astype(F32)).reshape(peers // 2, 8, 2 * half)
    turned = pltpu.roll(both, 4, 1)
    upper = lax.broadcasted_iota(jnp.int32, (peers // 2, 8, half), 1) < 4
    even = jnp.where(upper, both[:, :, :half], turned[:, :, half:])
    odd = jnp.where(upper, turned[:, :, :half], both[:, :, half:])
    joint = jnp.stack([even, odd], axis=1).reshape(peers, 8, half)
    out_ref[:, :, width:] = joint.astype(BF)


def finish_kernel(scale, slots_ref, arrived_ref, in_ref, out_ref, events_ref, new_in, new_out, spread_ref, rows_ref):
    peers, slots, _ = arrived_ref.shape
    count, width = events_ref.shape
    spread_ref[...] = spread_slots(slots_ref[...])
    rows_ref[...] = arrived_ref[:, :, :width].reshape(count, width)

    @pl.loop(0, count // TILE)
    def _(i):
        pick = slot_columns(spread_ref[rows_at(i), :], count)
        events_ref[rows_at(i), :] = dot(pick, rows_ref[...]).astype(BF)

    part = arrived_ref.shape[2] - width

    def add(i, sums):
        return tuple(
            total + arrived_ref[2 * i + core, :, width:].astype(F32) for core, total in enumerate(sums)
        )

    none = jnp.zeros((slots, part), F32)
    sums = lax.fori_loop(0, peers // 2, add, (none, none))
    pieces = [total[4 * h : 4 * h + 4] for total in sums for h in range(2)]
    total = jnp.concatenate(pieces, axis=1) * scale
    inner = in_ref.shape[1]
    new_in[...] = DECAY * in_ref[...] + total[:, :inner]
    new_out[...] = DECAY * out_ref[...] + total[:, inner:]


VMEM_SPEC = pl.BlockSpec(memory_space=pltpu.VMEM)
SMEM_SPEC = pl.BlockSpec(memory_space=pltpu.SMEM)


def place(slots, rows):
    count, width = rows.shape
    return pl.pallas_call(
        place_kernel,
        name="place_rows",
        out_shape=jax.ShapeDtypeStruct((count, width), BF),
        in_specs=[VMEM_SPEC] * 2,
        out_specs=VMEM_SPEC,
        cost_estimate=pl.CostEstimate(
            flops=2 * count * count * width, bytes_accessed=4 * count * width, transcendentals=0
        ),
    )(slots, rows)


def pack(rows, kept, got):
    peers, slots, width = rows.shape
    out = (peers, slots, width + kept.shape[1] // 2)
    return pl.pallas_call(
        pack_kernel,
        name="pack_rows",
        out_shape=jax.ShapeDtypeStruct(out, BF),
        in_specs=[VMEM_SPEC] * 3,
        out_specs=VMEM_SPEC,
        compiler_params=pltpu.CompilerParams(vmem_limit_bytes=32 << 20),
        cost_estimate=pl.CostEstimate(
            flops=kept.size, bytes_accessed=2 * 2 * (rows.size + kept.size), transcendentals=0
        ),
    )(rows, kept, got)


def finish(scale, slots, arrived, momentum_in, momentum_out):
    count, width = slots.shape[1], momentum_out.shape[1]
    return pl.pallas_call(
        functools.partial(finish_kernel, scale),
        name="finish_step",
        out_shape=(
            jax.ShapeDtypeStruct((count, width), BF),
            jax.ShapeDtypeStruct(momentum_in.shape, F32),
            jax.ShapeDtypeStruct(momentum_out.shape, F32),
        ),
        in_specs=[VMEM_SPEC] * 4,
        out_specs=(VMEM_SPEC,) * 3,
        scratch_shapes=[pltpu.VMEM((count, 128), jnp.int32), pltpu.VMEM((count, width), BF)],
        compiler_params=pltpu.CompilerParams(vmem_limit_bytes=32 << 20),
        cost_estimate=pl.CostEstimate(
            flops=2 * count * count * width, bytes_accessed=4 * count * width, transcendentals=0
        ),
    )(slots, arrived, momentum_in, momentum_out)


def layer(lens, dest, inbox, weights, upstream):
    count, width = inbox.shape
    tiles, pairs, far = count // TILE, width // 128, (count - BLK) // TILE
    return pl.pallas_call(
        layer_kernel,
        name="layer_step",
        out_shape=(
            jax.ShapeDtypeStruct((count, width), BF),
            jax.ShapeDtypeStruct((width, weights.shape[1] // 2), BF),
            jax.ShapeDtypeStruct((width, weights.shape[1] // 2), BF),
        ),
        in_specs=[SMEM_SPEC] + [VMEM_SPEC] * 4,
        out_specs=(VMEM_SPEC,) * 3,
        scratch_shapes=[
            pltpu.VMEM((count, 128), jnp.int32),
            pltpu.VMEM((width, count), BF),
            pltpu.VMEM((count, 4 * width), F32),
            pltpu.VMEM((count, width), F32),
            pltpu.VMEM((count, width), BF),
            pltpu.VMEM((count, width), BF),
            pltpu.VMEM((count, width), BF),
            pltpu.VMEM((count, width), F32),
            pltpu.VMEM((width, count), BF),
            pltpu.VMEM((count, width), BF),
            pltpu.VMEM((pairs, tiles, 2 * TILE, BLK), BF),
            pltpu.VMEM((pairs, tiles, 2 * TILE, BLK), BF),
            pltpu.VMEM((pairs, far, 2 * TILE, BLK), BF),
            pltpu.VMEM((pairs, far, 2 * TILE, BLK), BF),
            pltpu.VMEM((count, 128), F32),
            pltpu.VMEM((count, 128), F32),
            pltpu.VMEM((count, 4 * width), BF),
            pltpu.VMEM((count, width), BF),
        ],
        compiler_params=pltpu.CompilerParams(vmem_limit_bytes=60 << 20),
        cost_estimate=pl.CostEstimate(
            flops=30_000_000_000, bytes_accessed=12_000_000, transcendentals=10_000_000
        ),
    )(lens, dest, inbox, weights, upstream)


def shards(events, home_slot, dest_slot, seq_lens, weights, out_grad, momentum_in, momentum_out):
    row_count, model_width = events.shape
    home = home_slot.reshape(1, row_count)
    dest = dest_slot.reshape(1, row_count)
    peers = lax.axis_size(DP)
    slots = row_count // peers

    def exchange(blocks):
        return lax.all_to_all(blocks, DP, split_axis=0, concat_axis=0, tiled=True)

    outbox = place(home, events).reshape(peers, slots, model_width)
    inbox = exchange(outbox).reshape(row_count, model_width)
    sendback, kept, given = layer(seq_lens, dest, inbox, weights, out_grad)
    got = lax.ppermute(given, CORE, [(0, 1), (1, 0)])
    wire = pack(sendback.reshape(peers, slots, model_width), kept, got)
    grad_scale = (peers * row_count) ** (-0.5)
    return finish(grad_scale, home, exchange(wire), momentum_in, momentum_out)


def solution(mesh):
    split = Mesh(mesh.devices.reshape(4, 4, 4, 2), DP)
    return jax.shard_map(
        shards,
        mesh=split,
        in_specs=(P(DP, None), P(DP), P(DP), P(DP), P(), P(DP, None), P(DP, None), P(DP, None)),
        out_specs=(P(DP, None), P(DP, None), P(DP, None)),
        check_vma=False,
    )
```

```python
import functools

import jax
import jax.numpy as jnp
from jax import lax
from jax.experimental import pallas as pl
from jax.experimental.pallas import tpu as pltpu
from jax.sharding import Mesh
from jax.sharding import PartitionSpec as P

BLK = 512
DP = ("dp_0", "dp_1", "dp_2", "dp_3")
CHIPS = DP[:3]
CORE = DP[3]

NORM_EPS = 1e-05
DECAY = 0.9
TILE = 256
BF = jnp.bfloat16
F32 = jnp.float32


def dot(a, b):
    return jnp.dot(a, b, preferred_element_type=F32)


def dot_nt(a, b):
    return lax.dot_general(a, b, (((1,), (1,)), ((), ())), preferred_element_type=F32)


def dot_tn(a, b):
    return lax.dot_general(a, b, (((0,), (0,)), ((), ())), preferred_element_type=F32)


def rows_at(i):
    return pl.ds(pl.multiple_of(i * TILE, TILE), TILE)


def slot_rows(slots, first, count):
    places = lax.broadcasted_iota(jnp.int32, (count, slots.shape[1]), 0) + first
    return jnp.where(slots == places, 1.0, 0.0).astype(BF)


def slot_columns(spread, count):
    lane = lax.broadcasted_iota(jnp.int32, spread.shape, 1)
    parts = [
        jnp.where(spread == lane + at, 1.0, 0.0).astype(BF) for at in range(0, count, 128)
    ]
    return jnp.concatenate(parts, axis=1)


def spread_slots(slots):
    return jnp.transpose(jnp.broadcast_to(slots, (128, slots.shape[1])))


def place_kernel(slots_ref, rows_ref, out_ref):
    @pl.loop(0, out_ref.shape[0] // TILE)
    def _(i):
        pick = slot_rows(slots_ref[...], i * TILE, TILE)
        out_ref[rows_at(i), :] = dot(pick, rows_ref[...]).astype(BF)


def silu_parts(half):
    plus = 1.0 + jnp.tanh(half)
    value = half * plus
    return value, plus + value * (2.0 - plus)


def two_heads(rows):
    lane = lax.broadcasted_iota(jnp.int32, rows.shape, 1)
    none = jnp.zeros_like(rows)
    low = lane < 64
    return jnp.concatenate([jnp.where(low, rows, none), jnp.where(low, none, rows)], axis=0)


def own_lanes(stacked):
    half = stacked.shape[0] // 2
    lane = lax.broadcasted_iota(jnp.int32, (half, stacked.shape[1]), 1)
    return jnp.where(lane < 64, stacked[:half], stacked[half:])


def layer_kernel(
    lens_ref,
    dest_ref,
    inbox_ref,
    weights_ref,
    upstream_ref,
    sendback_ref,
    kept_ref,
    given_ref,
    spread_ref,
    tokens_t,
    slope,
    gate,
    vals,
    queries,
    keys,
    attended,
    mixed_t,
    att_grad,
    weights_kept,
    slopes_kept,
    key_sum,
    val_sum,
    hidden_grad,
    token_grad,
):
    row_count, width = inbox_ref.shape
    tiles = row_count // TILE
    pairs = width // 128
    first, second = lens_ref[0], lens_ref[1]
    joined = jnp.where(first > 0, first, second) > BLK
    spread_ref[...] = spread_slots(dest_ref[...])

    @pl.loop(0, tiles)
    def _(i):
        rows = rows_at(i)
        pick = slot_columns(spread_ref[rows, :], row_count)
        tokens = dot(pick, inbox_ref[...]).astype(BF)
        tokens_t[:, rows] = tokens.T
        for g in range(4):
            columns = slice(g * width, (g + 1) * width)
            half = dot(tokens, weights_ref[:, columns]) * 0.5
            value, slope2 = silu_parts(half)
            slope[rows, columns] = (0.5 * slope2).astype(BF)
            if g == 0:
                gate[rows, :] = value
            elif g == 1:
                vals[rows, :] = value.astype(BF)
            elif g == 2:
                queries[rows, :] = value.astype(BF) * jnp.asarray(0.0625, BF)
            else:
                keys[rows, :] = value.astype(BF)

    offsets = [sum(TILE * (t + 1) for t in range(i)) for i in range(tiles)]

    def forward_tile(p, i, low, high, edge):
        lanes = pl.ds(pl.multiple_of(p * 128, 128), 128)
        rows = slice(i * TILE, (i + 1) * TILE)
        kept = slice(offsets[i] + low, offsets[i] + high)
        stacked = two_heads(queries[rows, lanes])
        weight, slope2 = silu_parts(dot_nt(stacked, keys[low:high, lanes]))
        if edge:
            place = lax.broadcasted_iota(jnp.int32, (TILE, high - low), 0) + (i * TILE - low)
            seen = lax.broadcasted_iota(jnp.int32, (TILE, high - low), 1) <= place
            seen = jnp.concatenate([seen, seen], axis=0)
            weight = jnp.where(seen, weight, 0.0)
            slope2 = jnp.where(seen, slope2, 0.0)
        weight = weight.astype(BF)
        weights_kept[p, :, kept] = weight
        slopes_kept[p, :, kept] = slope2.astype(BF)
        return rows, lanes, own_lanes(dot(weight, vals[low:high, lanes]))

    @pl.loop(0, pairs)
    def _(p):
        for i in range(tiles):
            rows, lanes, part = forward_tile(p, i, i * TILE // BLK * BLK, (i + 1) * TILE, True)
            attended[rows, lanes] = part

    @pl.when(joined)
    def _():
        @pl.loop(0, pairs)
        def _(p):
            for i in range(BLK // TILE, tiles):
                rows, lanes, part = forward_tile(p, i, 0, BLK, False)
                attended[rows, lanes] += part

    def backward_pair(p, reach):
        start = pl.multiple_of(p * 128, 128)
        lanes = pl.ds(start, 128)
        key_sum[...] = jnp.zeros_like(key_sum)
        val_sum[...] = jnp.zeros_like(val_sum)
        for i in range(tiles):
            rows = slice(i * TILE, (i + 1) * TILE)
            stacked = two_heads(queries[rows, lanes])
            down = two_heads(att_grad[rows, lanes])
            low, high = (0 if reach else (i * TILE) // BLK * BLK), (i + 1) * TILE
            kept = slice(offsets[i] + low, offsets[i] + high)
            score = dot_nt(down, vals[low:high, lanes]).astype(BF) * slopes_kept[p, :, kept]
            val_sum[:, low:high] += dot(down.T, weights_kept[p, :, kept])
            key_sum[:, low:high] += dot(stacked.T, score)
            attended[rows, :128] = own_lanes(dot(score, keys[low:high, lanes]))
        for source, group, factor in (
            (val_sum[...].T, 1, 1.0),
            (attended[:, :128], 2, 0.0625),
            (key_sum[...].T, 3, 1.0),
        ):
            columns = pl.ds(pl.multiple_of(start + group * width, 128), 128)
            rounded = (source * factor).astype(BF).astype(F32)
            hidden_grad[:, columns] = (rounded * slope[:, columns].astype(F32)).astype(BF)

    def over_pairs(step):
        @pl.when(joined)
        def _():
            pl.loop(0, pairs)(lambda p: step(p, True))

        @pl.when(jnp.logical_not(joined))
        def _():
            pl.loop(0, pairs)(lambda p: step(p, False))

    @pl.loop(0, tiles)
    def _(i):
        rows = rows_at(i)
        value = attended[rows, :]
        centre = jnp.mean(value, axis=1, keepdims=True)
        centred = value - centre
        spread = jnp.mean(centred * centred, axis=1, keepdims=True)
        scale = lax.rsqrt(spread + NORM_EPS)
        normed = centred * scale
        gates = gate[rows, :]
        mixed_t[:, rows] = (normed * gates).astype(BF).T
        mixed_grad = dot_nt(upstream_ref[rows, :], weights_ref[:, 4 * width :])
        hidden_grad[rows, :width] = (mixed_grad * normed * slope[rows, :width].astype(F32)).astype(BF)
        down = mixed_grad * gates
        mean_down = jnp.mean(down, axis=1, keepdims=True)
        mean_both = jnp.mean(down * normed, axis=1, keepdims=True)
        att_grad[rows, :] = (scale * (down - mean_down - normed * mean_both)).astype(BF)

    over_pairs(backward_pair)

    @pl.loop(0, tiles)
    def _(i):
        rows = rows_at(i)
        total = dot_nt(hidden_grad[rows, :], weights_ref[:, : 4 * width])
        token_grad[rows, :] = (upstream_ref[rows, :].astype(F32) + total).astype(BF)

    @pl.loop(0, tiles)
    def _(i):
        pick = slot_rows(dest_ref[...], i * TILE, TILE)
        sendback_ref[rows_at(i), :] = dot(pick, token_grad[...]).astype(BF)

    halves = kept_ref.shape[1] // TILE
    ours = lax.axis_index(CORE)

    def put(value, i):
        half = i // halves
        columns = rows_at(i - half * halves)

        @pl.when(half == ours)
        def _():
            kept_ref[:, columns] = value

        @pl.when(half != ours)
        def _():
            given_ref[:, columns] = value

    inner = 4 * width // TILE

    @pl.loop(0, inner)
    def _(i):
        put(dot(tokens_t[...], hidden_grad[:, rows_at(i)]).astype(BF), i)

    for i in range(width // TILE):
        columns = slice(i * TILE, (i + 1) * TILE)
        put(dot(mixed_t[...], upstream_ref[:, columns]).astype(BF), inner + i)


def pack_kernel(rows_ref, kept_ref, got_ref, out_ref):
    peers, slots, width = rows_ref.shape
    half = kept_ref.shape[1] // 2
    out_ref[:, :, :width] = rows_ref[...]
    both = (kept_ref[...].astype(F32) + got_ref[...].astype(F32)).reshape(peers // 2, 8, 2 * half)
    turned = pltpu.roll(both, 4, 1)
    upper = lax.broadcasted_iota(jnp.int32, (peers // 2, 8, half), 1) < 4
    even = jnp.where(upper, both[:, :, :half], turned[:, :, half:])
    odd = jnp.where(upper, turned[:, :, :half], both[:, :, half:])
    joint = jnp.stack([even, odd], axis=1).reshape(peers, 8, half)
    out_ref[:, :, width:] = joint.astype(BF)


def finish_kernel(scale, slots_ref, arrived_ref, in_ref, out_ref, events_ref, new_in, new_out, spread_ref, rows_ref):
    peers, slots, _ = arrived_ref.shape
    count, width = events_ref.shape
    spread_ref[...] = spread_slots(slots_ref[...])
    rows_ref[...] = arrived_ref[:, :, :width].reshape(count, width)

    @pl.loop(0, count // TILE)
    def _(i):
        pick = slot_columns(spread_ref[rows_at(i), :], count)
        events_ref[rows_at(i), :] = dot(pick, rows_ref[...]).astype(BF)

    part = arrived_ref.shape[2] - width

    def add(i, sums):
        return tuple(
            total + arrived_ref[2 * i + core, :, width:].astype(F32) for core, total in enumerate(sums)
        )

    none = jnp.zeros((slots, part), F32)
    sums = lax.fori_loop(0, peers // 2, add, (none, none))
    pieces = [total[4 * h : 4 * h + 4] for total in sums for h in range(2)]
    total = jnp.concatenate(pieces, axis=1) * scale
    inner = in_ref.shape[1]
    new_in[...] = DECAY * in_ref[...] + total[:, :inner]
    new_out[...] = DECAY * out_ref[...] + total[:, inner:]


VMEM_SPEC = pl.BlockSpec(memory_space=pltpu.VMEM)
SMEM_SPEC = pl.BlockSpec(memory_space=pltpu.SMEM)


def place(slots, rows):
    count, width = rows.shape
    return pl.pallas_call(
        place_kernel,
        name="place_rows",
        out_shape=jax.ShapeDtypeStruct((count, width), BF),
        in_specs=[VMEM_SPEC] * 2,
        out_specs=VMEM_SPEC,
        cost_estimate=pl.CostEstimate(
            flops=2 * count * count * width, bytes_accessed=4 * count * width, transcendentals=0
        ),
    )(slots, rows)


def pack(rows, kept, got):
    peers, slots, width = rows.shape
    out = (peers, slots, width + kept.shape[1] // 2)
    return pl.pallas_call(
        pack_kernel,
        name="pack_rows",
        out_shape=jax.ShapeDtypeStruct(out, BF),
        in_specs=[VMEM_SPEC] * 3,
        out_specs=VMEM_SPEC,
        compiler_params=pltpu.CompilerParams(vmem_limit_bytes=32 << 20),
        cost_estimate=pl.CostEstimate(
            flops=kept.size, bytes_accessed=2 * 2 * (rows.size + kept.size), transcendentals=0
        ),
    )(rows, kept, got)


def finish(scale, slots, arrived, momentum_in, momentum_out):
    count, width = slots.shape[1], momentum_out.shape[1]
    return pl.pallas_call(
        functools.partial(finish_kernel, scale),
        name="finish_step",
        out_shape=(
            jax.ShapeDtypeStruct((count, width), BF),
            jax.ShapeDtypeStruct(momentum_in.shape, F32),
            jax.ShapeDtypeStruct(momentum_out.shape, F32),
        ),
        in_specs=[VMEM_SPEC] * 4,
        out_specs=(VMEM_SPEC,) * 3,
        scratch_shapes=[pltpu.VMEM((count, 128), jnp.int32), pltpu.VMEM((count, width), BF)],
        compiler_params=pltpu.CompilerParams(vmem_limit_bytes=32 << 20),
        cost_estimate=pl.CostEstimate(
            flops=2 * count * count * width, bytes_accessed=4 * count * width, transcendentals=0
        ),
    )(slots, arrived, momentum_in, momentum_out)


def layer(lens, dest, inbox, weights, upstream):
    count, width = inbox.shape
    tiles, pairs = count // TILE, width // 128
    kept = TILE * tiles * (tiles + 1) // 2
    return pl.pallas_call(
        layer_kernel,
        name="layer_step",
        out_shape=(
            jax.ShapeDtypeStruct((count, width), BF),
            jax.ShapeDtypeStruct((width, weights.shape[1] // 2), BF),
            jax.ShapeDtypeStruct((width, weights.shape[1] // 2), BF),
        ),
        in_specs=[SMEM_SPEC] + [VMEM_SPEC] * 4,
        out_specs=(VMEM_SPEC,) * 3,
        scratch_shapes=[
            pltpu.VMEM((count, 128), jnp.int32),
            pltpu.VMEM((width, count), BF),
            pltpu.VMEM((count, 4 * width), BF),
            pltpu.VMEM((count, width), F32),
            pltpu.VMEM((count, width), BF),
            pltpu.VMEM((count, width), BF),
            pltpu.VMEM((count, width), BF),
            pltpu.VMEM((count, width), F32),
            pltpu.VMEM((width, count), BF),
            pltpu.VMEM((count, width), BF),
            pltpu.VMEM((pairs, 2 * TILE, kept), BF),
            pltpu.VMEM((pairs, 2 * TILE, kept), BF),
            pltpu.VMEM((128, count), F32),
            pltpu.VMEM((128, count), F32),
            pltpu.VMEM((count, 4 * width), BF),
            pltpu.VMEM((count, width), BF),
        ],
        compiler_params=pltpu.CompilerParams(vmem_limit_bytes=44 << 20),
        cost_estimate=pl.CostEstimate(
            flops=30_000_000_000, bytes_accessed=12_000_000, transcendentals=10_000_000
        ),
    )(lens, dest, inbox, weights, upstream)


def shards(events, home_slot, dest_slot, seq_lens, weights, out_grad, momentum_in, momentum_out):
    row_count, model_width = events.shape
    home = home_slot.reshape(1, row_count)
    dest = dest_slot.reshape(1, row_count)
    peers = lax.axis_size(DP)
    slots = row_count // peers

    def exchange(blocks):
        return lax.all_to_all(blocks, DP, split_axis=0, concat_axis=0, tiled=True)

    outbox = place(home, events).reshape(peers, slots, model_width)
    inbox = exchange(outbox).reshape(row_count, model_width)
    sendback, kept, given = layer(seq_lens, dest, inbox, weights, out_grad)
    got = lax.ppermute(given, CORE, [(0, 1), (1, 0)])
    wire = pack(sendback.reshape(peers, slots, model_width), kept, got)
    grad_scale = (peers * row_count) ** (-0.5)
    return finish(grad_scale, home, exchange(wire), momentum_in, momentum_out)


def solution(mesh):
    split = Mesh(mesh.devices.reshape(4, 4, 4, 2), DP)
    return jax.shard_map(
        shards,
        mesh=split,
        in_specs=(P(DP, None), P(DP), P(DP), P(DP), P(), P(DP, None), P(DP, None), P(DP, None)),
        out_specs=(P(DP, None), P(DP, None), P(DP, None)),
        check_vma=False,
    )
```

```python
import functools

import jax
import jax.numpy as jnp
from jax import lax
from jax.experimental import pallas as pl
from jax.experimental.pallas import tpu as pltpu
from jax.sharding import Mesh
from jax.sharding import PartitionSpec as P

BLK = 512
DP = ("dp_0", "dp_1", "dp_2", "dp_3")
CHIPS = DP[:3]
CORE = DP[3]

NORM_EPS = 1e-05
DECAY = 0.9
TILE = 256
WIDE = 512
BF = jnp.bfloat16
F32 = jnp.float32


def dot(a, b):
    return jnp.dot(a, b, preferred_element_type=F32)


def dot_nt(a, b):
    return lax.dot_general(a, b, (((1,), (1,)), ((), ())), preferred_element_type=F32)


def dot_tn(a, b):
    return lax.dot_general(a, b, (((0,), (0,)), ((), ())), preferred_element_type=F32)


def rows_at(i, size=TILE):
    return pl.ds(pl.multiple_of(i * size, size), size)


def slot_rows(slots, first, count):
    places = lax.broadcasted_iota(jnp.int32, (count, slots.shape[1]), 0) + first
    return jnp.where(slots == places, 1.0, 0.0).astype(BF)


def slot_columns(spread, count):
    lane = lax.broadcasted_iota(jnp.int32, spread.shape, 1)
    parts = [
        jnp.where(spread == lane + at, 1.0, 0.0).astype(BF) for at in range(0, count, 128)
    ]
    return jnp.concatenate(parts, axis=1)


def spread_slots(slots):
    return jnp.transpose(jnp.broadcast_to(slots, (128, slots.shape[1])))


def place_kernel(slots_ref, rows_ref, out_ref):
    @pl.loop(0, out_ref.shape[0] // TILE)
    def _(i):
        pick = slot_rows(slots_ref[...], i * TILE, TILE)
        out_ref[rows_at(i), :] = dot(pick, rows_ref[...]).astype(BF)


def silu_parts(half):
    plus = 1.0 + jnp.tanh(half)
    value = half * plus
    return value, plus + value * (2.0 - plus)


def two_heads(rows):
    lane = lax.broadcasted_iota(jnp.int32, rows.shape, 1)
    none = jnp.zeros_like(rows)
    low = lane < 64
    return jnp.concatenate([jnp.where(low, rows, none), jnp.where(low, none, rows)], axis=0)


def own_lanes(stacked):
    half = stacked.shape[0] // 2
    lane = lax.broadcasted_iota(jnp.int32, (half, stacked.shape[1]), 1)
    return jnp.where(lane < 64, stacked[:half], stacked[half:])


def layer_kernel(
    lens_ref,
    dest_ref,
    inbox_ref,
    weights_ref,
    upstream_ref,
    hidden_grad,
    kept_ref,
    given_ref,
    spread_ref,
    tokens_t,
    slope,
    gate,
    vals,
    queries,
    keys,
    attended,
    mixed_t,
    att_grad,
    weights_kept,
    slopes_kept,
    key_sum,
    val_sum,
):
    row_count, width = inbox_ref.shape
    tiles = row_count // TILE
    pairs = width // 128
    first, second = lens_ref[0], lens_ref[1]
    joined = jnp.where(first > 0, first, second) > BLK
    spread_ref[...] = spread_slots(dest_ref[...])

    @pl.loop(0, row_count // WIDE)
    def _(i):
        rows = rows_at(i, WIDE)
        pick = slot_columns(spread_ref[rows, :], row_count)
        tokens = dot(pick, inbox_ref[...]).astype(BF)
        tokens_t[:, rows] = tokens.T
        for g in range(4):
            columns = slice(g * width, (g + 1) * width)
            half = dot(tokens, weights_ref[:, columns]) * 0.5
            value, slope2 = silu_parts(half)
            slope[rows, columns] = (0.5 * slope2).astype(BF)
            if g == 0:
                gate[rows, :] = value
            elif g == 1:
                vals[rows, :] = value.astype(BF)
            elif g == 2:
                queries[rows, :] = value.astype(BF) * jnp.asarray(0.0625, BF)
            else:
                keys[rows, :] = value.astype(BF)

    offsets = [sum(TILE * (t + 1) for t in range(i)) for i in range(tiles)]

    def forward_tile(p, i, low, high, edge):
        lanes = pl.ds(pl.multiple_of(p * 128, 128), 128)
        rows = slice(i * TILE, (i + 1) * TILE)
        kept = slice(offsets[i] + low, offsets[i] + high)
        stacked = two_heads(queries[rows, lanes])
        half = dot_nt(stacked, keys[low:high, lanes])
        plus = 1.0 + jnp.tanh(half)
        weight = (half * plus).astype(BF)
        plus = plus.astype(BF)
        slope2 = plus + weight * (2.0 - plus)
        if edge:
            place = lax.broadcasted_iota(jnp.int32, (TILE, high - low), 0) + (i * TILE - low)
            seen = lax.broadcasted_iota(jnp.int32, (TILE, high - low), 1) <= place
            seen = jnp.concatenate([seen, seen], axis=0)
            none = jnp.zeros_like(weight)
            weight = jnp.where(seen, weight, none)
            slope2 = jnp.where(seen, slope2, none)
        weights_kept[p, :, kept] = weight
        slopes_kept[p, :, kept] = slope2
        return rows, lanes, own_lanes(dot(weight, vals[low:high, lanes]))

    @pl.loop(0, pairs)
    def _(p):
        for i in range(tiles):
            rows, lanes, part = forward_tile(p, i, i * TILE // BLK * BLK, (i + 1) * TILE, True)
            attended[rows, lanes] = part

    @pl.when(joined)
    def _():
        @pl.loop(0, pairs)
        def _(p):
            for i in range(BLK // TILE, tiles):
                rows, lanes, part = forward_tile(p, i, 0, BLK, False)
                attended[rows, lanes] += part

    def backward_pair(p, reach):
        start = pl.multiple_of(p * 128, 128)
        lanes = pl.ds(start, 128)
        key_sum[...] = jnp.zeros_like(key_sum)
        val_sum[...] = jnp.zeros_like(val_sum)
        for i in range(tiles):
            rows = slice(i * TILE, (i + 1) * TILE)
            stacked = two_heads(queries[rows, lanes])
            down = two_heads(att_grad[rows, lanes])
            low, high = (0 if reach else (i * TILE) // BLK * BLK), (i + 1) * TILE
            kept = slice(offsets[i] + low, offsets[i] + high)
            score = dot_nt(down, vals[low:high, lanes]).astype(BF) * slopes_kept[p, :, kept]
            val_sum[:, low:high] += dot(down.T, weights_kept[p, :, kept])
            key_sum[:, low:high] += dot(stacked.T, score)
            attended[rows, :128] = own_lanes(dot(score, keys[low:high, lanes]))
        for source, group, factor in (
            (val_sum[...].T, 1, 1.0),
            (attended[:, :128], 2, 0.0625),
            (key_sum[...].T, 3, 1.0),
        ):
            columns = pl.ds(pl.multiple_of(start + group * width, 128), 128)
            rounded = (source * factor).astype(BF).astype(F32)
            hidden_grad[:, columns] = (rounded * slope[:, columns].astype(F32)).astype(BF)

    def over_pairs(step):
        @pl.when(joined)
        def _():
            pl.loop(0, pairs)(lambda p: step(p, True))

        @pl.when(jnp.logical_not(joined))
        def _():
            pl.loop(0, pairs)(lambda p: step(p, False))

    @pl.loop(0, tiles)
    def _(i):
        rows = rows_at(i)
        value = attended[rows, :]
        centre = jnp.mean(value, axis=1, keepdims=True)
        centred = value - centre
        spread = jnp.mean(centred * centred, axis=1, keepdims=True)
        scale = lax.rsqrt(spread + NORM_EPS)
        normed = centred * scale
        gates = gate[rows, :]
        mixed_t[:, rows] = (normed * gates).astype(BF).T
        mixed_grad = dot_nt(upstream_ref[rows, :], weights_ref[:, 4 * width :])
        hidden_grad[rows, :width] = (mixed_grad * normed * slope[rows, :width].astype(F32)).astype(BF)
        down = mixed_grad * gates
        mean_down = jnp.mean(down, axis=1, keepdims=True)
        mean_both = jnp.mean(down * normed, axis=1, keepdims=True)
        att_grad[rows, :] = (scale * (down - mean_down - normed * mean_both)).astype(BF)

    over_pairs(backward_pair)

    halves = kept_ref.shape[1] // TILE
    ours = lax.axis_index(CORE)

    def put(value, i):
        half = i // halves
        columns = rows_at(i - half * halves)

        @pl.when(half == ours)
        def _():
            kept_ref[:, columns] = value

        @pl.when(half != ours)
        def _():
            given_ref[:, columns] = value

    inner = 4 * width // TILE

    @pl.loop(0, inner)
    def _(i):
        put(dot(tokens_t[...], hidden_grad[:, rows_at(i)]).astype(BF), i)

    for i in range(width // TILE):
        columns = slice(i * TILE, (i + 1) * TILE)
        put(dot(mixed_t[...], upstream_ref[:, columns]).astype(BF), inner + i)


def back_kernel(dest_ref, hidden_grad, weights_ref, upstream_ref, sendback_ref, token_grad):
    row_count, width = upstream_ref.shape

    @pl.loop(0, row_count // WIDE)
    def _(i):
        rows = rows_at(i, WIDE)
        total = dot_nt(hidden_grad[rows, :], weights_ref[:, : 4 * width])
        token_grad[rows, :] = (upstream_ref[rows, :].astype(F32) + total).astype(BF)

    @pl.loop(0, row_count // WIDE)
    def _(i):
        pick = slot_rows(dest_ref[...], i * WIDE, WIDE)
        sendback_ref[rows_at(i, WIDE), :] = dot(pick, token_grad[...]).astype(BF)


def pack_kernel(rows_ref, kept_ref, got_ref, out_ref):
    peers, slots, width = rows_ref.shape
    half = kept_ref.shape[1] // 2
    out_ref[:, :, :width] = rows_ref[...]
    both = (kept_ref[...].astype(F32) + got_ref[...].astype(F32)).reshape(peers // 2, 8, 2 * half)
    turned = pltpu.roll(both, 4, 1)
    upper = lax.broadcasted_iota(jnp.int32, (peers // 2, 8, half), 1) < 4
    even = jnp.where(upper, both[:, :, :half], turned[:, :, half:])
    odd = jnp.where(upper, turned[:, :, :half], both[:, :, half:])
    joint = jnp.stack([even, odd], axis=1).reshape(peers, 8, half)
    out_ref[:, :, width:] = joint.astype(BF)


def finish_kernel(scale, slots_ref, arrived_ref, in_ref, out_ref, events_ref, new_in, new_out, spread_ref, rows_ref):
    peers, slots, _ = arrived_ref.shape
    count, width = events_ref.shape
    spread_ref[...] = spread_slots(slots_ref[...])
    rows_ref[...] = arrived_ref[:, :, :width].reshape(count, width)

    @pl.loop(0, count // TILE)
    def _(i):
        pick = slot_columns(spread_ref[rows_at(i), :], count)
        events_ref[rows_at(i), :] = dot(pick, rows_ref[...]).astype(BF)

    part = arrived_ref.shape[2] - width

    def add(i, sums):
        return tuple(
            total + arrived_ref[2 * i + core, :, width:].astype(F32) for core, total in enumerate(sums)
        )

    none = jnp.zeros((slots, part), F32)
    sums = lax.fori_loop(0, peers // 2, add, (none, none))
    pieces = [total[4 * h : 4 * h + 4] for total in sums for h in range(2)]
    total = jnp.concatenate(pieces, axis=1) * scale
    inner = in_ref.shape[1]
    new_in[...] = DECAY * in_ref[...] + total[:, :inner]
    new_out[...] = DECAY * out_ref[...] + total[:, inner:]


VMEM_SPEC = pl.BlockSpec(memory_space=pltpu.VMEM)
SMEM_SPEC = pl.BlockSpec(memory_space=pltpu.SMEM)


def place(slots, rows):
    count, width = rows.shape
    return pl.pallas_call(
        place_kernel,
        name="place_rows",
        out_shape=jax.ShapeDtypeStruct((count, width), BF),
        in_specs=[VMEM_SPEC] * 2,
        out_specs=VMEM_SPEC,
        cost_estimate=pl.CostEstimate(
            flops=2 * count * count * width, bytes_accessed=4 * count * width, transcendentals=0
        ),
    )(slots, rows)


def back(dest, hidden_grad, weights, upstream):
    count, width = upstream.shape
    return pl.pallas_call(
        back_kernel,
        name="back_rows",
        out_shape=jax.ShapeDtypeStruct((count, width), BF),
        in_specs=[VMEM_SPEC] * 4,
        out_specs=VMEM_SPEC,
        scratch_shapes=[pltpu.VMEM((count, width), BF)],
        compiler_params=pltpu.CompilerParams(vmem_limit_bytes=20 << 20),
        cost_estimate=pl.CostEstimate(
            flops=10 * count * width * width, bytes_accessed=10_000_000, transcendentals=0
        ),
    )(dest, hidden_grad, weights, upstream)


def pack(rows, kept, got):
    peers, slots, width = rows.shape
    out = (peers, slots, width + kept.shape[1] // 2)
    return pl.pallas_call(
        pack_kernel,
        name="pack_rows",
        out_shape=jax.ShapeDtypeStruct(out, BF),
        in_specs=[VMEM_SPEC] * 3,
        out_specs=VMEM_SPEC,
        compiler_params=pltpu.CompilerParams(vmem_limit_bytes=32 << 20),
        cost_estimate=pl.CostEstimate(
            flops=kept.size, bytes_accessed=2 * 2 * (rows.size + kept.size), transcendentals=0
        ),
    )(rows, kept, got)


def finish(scale, slots, arrived, momentum_in, momentum_out):
    count, width = slots.shape[1], momentum_out.shape[1]
    return pl.pallas_call(
        functools.partial(finish_kernel, scale),
        name="finish_step",
        out_shape=(
            jax.ShapeDtypeStruct((count, width), BF),
            jax.ShapeDtypeStruct(momentum_in.shape, F32),
            jax.ShapeDtypeStruct(momentum_out.shape, F32),
        ),
        in_specs=[VMEM_SPEC] * 4,
        out_specs=(VMEM_SPEC,) * 3,
        scratch_shapes=[pltpu.VMEM((count, 128), jnp.int32), pltpu.VMEM((count, width), BF)],
        compiler_params=pltpu.CompilerParams(vmem_limit_bytes=32 << 20),
        cost_estimate=pl.CostEstimate(
            flops=2 * count * count * width, bytes_accessed=4 * count * width, transcendentals=0
        ),
    )(slots, arrived, momentum_in, momentum_out)


def layer(lens, dest, inbox, weights, upstream):
    count, width = inbox.shape
    tiles, pairs = count // TILE, width // 128
    kept = TILE * tiles * (tiles + 1) // 2
    return pl.pallas_call(
        layer_kernel,
        name="layer_step",
        out_shape=(
            jax.ShapeDtypeStruct((count, 4 * width), BF),
            jax.ShapeDtypeStruct((width, weights.shape[1] // 2), BF),
            jax.ShapeDtypeStruct((width, weights.shape[1] // 2), BF),
        ),
        in_specs=[SMEM_SPEC] + [VMEM_SPEC] * 4,
        out_specs=(VMEM_SPEC,) * 3,
        scratch_shapes=[
            pltpu.VMEM((count, 128), jnp.int32),
            pltpu.VMEM((width, count), BF),
            pltpu.VMEM((count, 4 * width), BF),
            pltpu.VMEM((count, width), F32),
            pltpu.VMEM((count, width), BF),
            pltpu.VMEM((count, width), BF),
            pltpu.VMEM((count, width), BF),
            pltpu.VMEM((count, width), F32),
            pltpu.VMEM((width, count), BF),
            pltpu.VMEM((count, width), BF),
            pltpu.VMEM((pairs, 2 * TILE, kept), BF),
            pltpu.VMEM((pairs, 2 * TILE, kept), BF),
            pltpu.VMEM((128, count), F32),
            pltpu.VMEM((128, count), F32),
        ],
        compiler_params=pltpu.CompilerParams(vmem_limit_bytes=41 << 20),
        cost_estimate=pl.CostEstimate(
            flops=30_000_000_000, bytes_accessed=12_000_000, transcendentals=10_000_000
        ),
    )(lens, dest, inbox, weights, upstream)


def shards(events, home_slot, dest_slot, seq_lens, weights, out_grad, momentum_in, momentum_out):
    row_count, model_width = events.shape
    home = home_slot.reshape(1, row_count)
    dest = dest_slot.reshape(1, row_count)
    peers = lax.axis_size(DP)
    slots = row_count // peers

    def exchange(blocks):
        return lax.all_to_all(blocks, DP, split_axis=0, concat_axis=0, tiled=True)

    outbox = place(home, events).reshape(peers, slots, model_width)
    inbox = exchange(outbox).reshape(row_count, model_width)
    hidden_grad, kept, given = layer(seq_lens, dest, inbox, weights, out_grad)
    got = lax.ppermute(given, CORE, [(0, 1), (1, 0)])
    sendback = back(dest, hidden_grad, weights, out_grad)
    wire = pack(sendback.reshape(peers, slots, model_width), kept, got)
    grad_scale = (peers * row_count) ** (-0.5)
    return finish(grad_scale, home, exchange(wire), momentum_in, momentum_out)


def solution(mesh):
    split = Mesh(mesh.devices.reshape(4, 4, 4, 2), DP)
    return jax.shard_map(
        shards,
        mesh=split,
        in_specs=(P(DP, None), P(DP), P(DP), P(DP), P(), P(DP, None), P(DP, None), P(DP, None)),
        out_specs=(P(DP, None), P(DP, None), P(DP, None)),
        check_vma=False,
    )
```

```python
import functools

import jax
import jax.numpy as jnp
from jax import lax
from jax.experimental import pallas as pl
from jax.experimental.pallas import tpu as pltpu
from jax.sharding import Mesh
from jax.sharding import PartitionSpec as P

BLK = 512
DP = ("dp_0", "dp_1", "dp_2", "dp_3")
CHIPS = DP[:3]
CORE = DP[3]

NORM_EPS = 1e-05
DECAY = 0.9
TILE = 256
WIDE = 512
BF = jnp.bfloat16
F32 = jnp.float32


def dot(a, b):
    return jnp.dot(a, b, preferred_element_type=F32)


def dot_nt(a, b):
    return lax.dot_general(a, b, (((1,), (1,)), ((), ())), preferred_element_type=F32)


def dot_tn(a, b):
    return lax.dot_general(a, b, (((0,), (0,)), ((), ())), preferred_element_type=F32)


def rows_at(i, size=TILE):
    return pl.ds(pl.multiple_of(i * size, size), size)


def slot_rows(slots, first, count):
    places = lax.broadcasted_iota(jnp.int32, (count, slots.shape[1]), 0) + first
    return jnp.where(slots == places, 1.0, 0.0).astype(BF)


def slot_columns(spread, count):
    lane = lax.broadcasted_iota(jnp.int32, spread.shape, 1)
    parts = [
        jnp.where(spread == lane + at, 1.0, 0.0).astype(BF) for at in range(0, count, 128)
    ]
    return jnp.concatenate(parts, axis=1)


def spread_slots(slots):
    return jnp.transpose(jnp.broadcast_to(slots, (128, slots.shape[1])))


def place_kernel(slots_ref, rows_ref, out_ref):
    @pl.loop(0, out_ref.shape[0] // WIDE)
    def _(i):
        pick = slot_rows(slots_ref[...], i * WIDE, WIDE)
        out_ref[rows_at(i, WIDE), :] = dot(pick, rows_ref[...]).astype(BF)


def silu_parts(half):
    plus = 1.0 + jnp.tanh(half)
    value = half * plus
    return value, plus + value * (2.0 - plus)


def two_heads(rows):
    lane = lax.broadcasted_iota(jnp.int32, rows.shape, 1)
    none = jnp.zeros_like(rows)
    low = lane < 64
    return jnp.concatenate([jnp.where(low, rows, none), jnp.where(low, none, rows)], axis=0)


def own_lanes(stacked):
    half = stacked.shape[0] // 2
    lane = lax.broadcasted_iota(jnp.int32, (half, stacked.shape[1]), 1)
    return jnp.where(lane < 64, stacked[:half], stacked[half:])


def layer_kernel(
    lens_ref,
    dest_ref,
    inbox_ref,
    weights_ref,
    upstream_ref,
    hidden_grad,
    kept_ref,
    given_ref,
    spread_ref,
    tokens_t,
    gate,
    vals,
    queries,
    keys,
    attended,
    mixed_t,
    att_grad,
    weights_kept,
    slopes_kept,
    key_sum,
    val_sum,
):
    row_count, width = inbox_ref.shape
    tiles = row_count // TILE
    pairs = width // 128
    first, second = lens_ref[0], lens_ref[1]
    joined = jnp.where(first > 0, first, second) > BLK
    spread_ref[...] = spread_slots(dest_ref[...])

    @pl.loop(0, row_count // WIDE)
    def _(i):
        rows = rows_at(i, WIDE)
        pick = slot_columns(spread_ref[rows, :], row_count)
        tokens = dot(pick, inbox_ref[...]).astype(BF)
        tokens_t[:, rows] = tokens.T
        for g in range(4):
            columns = slice(g * width, (g + 1) * width)
            half = dot(tokens, weights_ref[:, columns]) * 0.5
            value, slope2 = silu_parts(half)
            hidden_grad[rows, columns] = (0.5 * slope2).astype(BF)
            if g == 0:
                gate[rows, :] = value
            elif g == 1:
                vals[rows, :] = value.astype(BF)
            elif g == 2:
                queries[rows, :] = value.astype(BF) * jnp.asarray(0.0625, BF)
            else:
                keys[rows, :] = value.astype(BF)

    offsets = [sum(TILE * (t + 1) for t in range(i)) for i in range(tiles)]

    def forward_tile(p, i, low, high, edge):
        lanes = pl.ds(pl.multiple_of(p * 128, 128), 128)
        rows = slice(i * TILE, (i + 1) * TILE)
        kept = slice(offsets[i] + low, offsets[i] + high)
        stacked = two_heads(queries[rows, lanes])
        half = dot_nt(stacked, keys[low:high, lanes])
        plus = 1.0 + jnp.tanh(half)
        weight = (half * plus).astype(BF)
        plus = plus.astype(BF)
        slope2 = plus + weight * (2.0 - plus)
        if edge:
            place = lax.broadcasted_iota(jnp.int32, (TILE, high - low), 0) + (i * TILE - low)
            seen = lax.broadcasted_iota(jnp.int32, (TILE, high - low), 1) <= place
            seen = jnp.concatenate([seen, seen], axis=0)
            none = jnp.zeros_like(weight)
            weight = jnp.where(seen, weight, none)
            slope2 = jnp.where(seen, slope2, none)
        weights_kept[p, :, kept] = weight
        slopes_kept[p, :, kept] = slope2
        return rows, lanes, own_lanes(dot(weight, vals[low:high, lanes]))

    @pl.loop(0, pairs)
    def _(p):
        for i in range(tiles):
            rows, lanes, part = forward_tile(p, i, i * TILE // BLK * BLK, (i + 1) * TILE, True)
            attended[rows, lanes] = part

    @pl.when(joined)
    def _():
        @pl.loop(0, pairs)
        def _(p):
            for i in range(BLK // TILE, tiles):
                rows, lanes, part = forward_tile(p, i, 0, BLK, False)
                attended[rows, lanes] += part

    def backward_pair(p, reach):
        start = pl.multiple_of(p * 128, 128)
        lanes = pl.ds(start, 128)
        key_sum[...] = jnp.zeros_like(key_sum)
        val_sum[...] = jnp.zeros_like(val_sum)
        for i in range(tiles):
            rows = slice(i * TILE, (i + 1) * TILE)
            stacked = two_heads(queries[rows, lanes])
            down = two_heads(att_grad[rows, lanes])
            low, high = (0 if reach else (i * TILE) // BLK * BLK), (i + 1) * TILE
            kept = slice(offsets[i] + low, offsets[i] + high)
            score = dot_nt(down, vals[low:high, lanes]).astype(BF) * slopes_kept[p, :, kept]
            val_sum[:, low:high] += dot(down.T, weights_kept[p, :, kept])
            key_sum[:, low:high] += dot(stacked.T, score)
            attended[rows, :128] = own_lanes(dot(score, keys[low:high, lanes]))
        for source, group, factor in (
            (val_sum[...].T, 1, 1.0),
            (attended[:, :128], 2, 0.0625),
            (key_sum[...].T, 3, 1.0),
        ):
            columns = pl.ds(pl.multiple_of(start + group * width, 128), 128)
            rounded = (source * factor).astype(BF).astype(F32)
            hidden_grad[:, columns] = (rounded * hidden_grad[:, columns].astype(F32)).astype(BF)

    def over_pairs(step):
        @pl.when(joined)
        def _():
            pl.loop(0, pairs)(lambda p: step(p, True))

        @pl.when(jnp.logical_not(joined))
        def _():
            pl.loop(0, pairs)(lambda p: step(p, False))

    @pl.loop(0, tiles)
    def _(i):
        rows = rows_at(i)
        value = attended[rows, :]
        centre = jnp.mean(value, axis=1, keepdims=True)
        centred = value - centre
        spread = jnp.mean(centred * centred, axis=1, keepdims=True)
        scale = lax.rsqrt(spread + NORM_EPS)
        normed = centred * scale
        gates = gate[rows, :]
        mixed_t[:, rows] = (normed * gates).astype(BF).T
        mixed_grad = dot_nt(upstream_ref[rows, :], weights_ref[:, 4 * width :])
        hidden_grad[rows, :width] = (mixed_grad * normed * hidden_grad[rows, :width].astype(F32)).astype(BF)
        down = mixed_grad * gates
        mean_down = jnp.mean(down, axis=1, keepdims=True)
        mean_both = jnp.mean(down * normed, axis=1, keepdims=True)
        att_grad[rows, :] = (scale * (down - mean_down - normed * mean_both)).astype(BF)

    over_pairs(backward_pair)

    ours = lax.axis_index(CORE)
    halves = kept_ref.shape[1] // TILE
    inner = 4 * width // TILE - halves

    def write_half(half, ref):
        @pl.loop(0, inner if half else halves)
        def _(i):
            columns = hidden_grad[:, rows_at(i + half * halves)]
            ref[:, rows_at(i)] = dot(tokens_t[...], columns).astype(BF)

        if half:
            ref[:, inner * TILE :] = dot(mixed_t[...], upstream_ref[...]).astype(BF)

    for core in range(2):

        @pl.when(ours == core)
        def _(core=core):
            write_half(core, kept_ref)
            write_half(1 - core, given_ref)


def back_kernel(dest_ref, hidden_grad, weights_ref, upstream_ref, sendback_ref, token_grad):
    row_count, width = upstream_ref.shape

    @pl.loop(0, row_count // WIDE)
    def _(i):
        rows = rows_at(i, WIDE)
        total = dot_nt(hidden_grad[rows, :], weights_ref[:, : 4 * width])
        token_grad[rows, :] = (upstream_ref[rows, :].astype(F32) + total).astype(BF)

    @pl.loop(0, row_count // WIDE)
    def _(i):
        pick = slot_rows(dest_ref[...], i * WIDE, WIDE)
        sendback_ref[rows_at(i, WIDE), :] = dot(pick, token_grad[...]).astype(BF)


def pack_kernel(rows_ref, kept_ref, got_ref, out_ref):
    peers, slots, width = rows_ref.shape
    half = kept_ref.shape[1] // 2
    out_ref[:, :, :width] = rows_ref[...]
    both = (kept_ref[...].astype(F32) + got_ref[...].astype(F32)).reshape(peers // 2, 8, 2 * half)
    turned = pltpu.roll(both, 4, 1)
    upper = lax.broadcasted_iota(jnp.int32, (peers // 2, 8, half), 1) < 4
    even = jnp.where(upper, both[:, :, :half], turned[:, :, half:])
    odd = jnp.where(upper, turned[:, :, :half], both[:, :, half:])
    joint = jnp.stack([even, odd], axis=1).reshape(peers, 8, half)
    out_ref[:, :, width:] = joint.astype(BF)


def finish_kernel(scale, slots_ref, arrived_ref, in_ref, out_ref, events_ref, new_in, new_out, spread_ref, rows_ref):
    peers, slots, _ = arrived_ref.shape
    count, width = events_ref.shape
    spread_ref[...] = spread_slots(slots_ref[...])
    rows_ref[...] = arrived_ref[:, :, :width].reshape(count, width)

    @pl.loop(0, count // WIDE)
    def _(i):
        rows = rows_at(i, WIDE)
        pick = slot_columns(spread_ref[rows, :], count)
        events_ref[rows, :] = dot(pick, rows_ref[...]).astype(BF)

    part = arrived_ref.shape[2] - width

    def add(i, sums):
        return tuple(
            total + arrived_ref[2 * i + core, :, width:].astype(F32) for core, total in enumerate(sums)
        )

    none = jnp.zeros((slots, part), F32)
    sums = lax.fori_loop(0, peers // 2, add, (none, none))
    pieces = [total[4 * h : 4 * h + 4] for total in sums for h in range(2)]
    total = jnp.concatenate(pieces, axis=1) * scale
    inner = in_ref.shape[1]
    new_in[...] = DECAY * in_ref[...] + total[:, :inner]
    new_out[...] = DECAY * out_ref[...] + total[:, inner:]


VMEM_SPEC = pl.BlockSpec(memory_space=pltpu.VMEM)
SMEM_SPEC = pl.BlockSpec(memory_space=pltpu.SMEM)


def place(slots, rows):
    count, width = rows.shape
    return pl.pallas_call(
        place_kernel,
        name="place_rows",
        out_shape=jax.ShapeDtypeStruct((count, width), BF),
        in_specs=[VMEM_SPEC] * 2,
        out_specs=VMEM_SPEC,
        compiler_params=pltpu.CompilerParams(vmem_limit_bytes=12 << 20),
        cost_estimate=pl.CostEstimate(
            flops=2 * count * count * width, bytes_accessed=4 * count * width, transcendentals=0
        ),
    )(slots, rows)


def back(dest, hidden_grad, weights, upstream):
    count, width = upstream.shape
    return pl.pallas_call(
        back_kernel,
        name="back_rows",
        out_shape=jax.ShapeDtypeStruct((count, width), BF),
        in_specs=[VMEM_SPEC] * 4,
        out_specs=VMEM_SPEC,
        scratch_shapes=[pltpu.VMEM((count, width), BF)],
        compiler_params=pltpu.CompilerParams(vmem_limit_bytes=20 << 20),
        cost_estimate=pl.CostEstimate(
            flops=10 * count * width * width, bytes_accessed=10_000_000, transcendentals=0
        ),
    )(dest, hidden_grad, weights, upstream)


def pack(rows, kept, got):
    peers, slots, width = rows.shape
    out = (peers, slots, width + kept.shape[1] // 2)
    return pl.pallas_call(
        pack_kernel,
        name="pack_rows",
        out_shape=jax.ShapeDtypeStruct(out, BF),
        in_specs=[VMEM_SPEC] * 3,
        out_specs=VMEM_SPEC,
        compiler_params=pltpu.CompilerParams(vmem_limit_bytes=32 << 20),
        cost_estimate=pl.CostEstimate(
            flops=kept.size, bytes_accessed=2 * 2 * (rows.size + kept.size), transcendentals=0
        ),
    )(rows, kept, got)


def finish(scale, slots, arrived, momentum_in, momentum_out):
    count, width = slots.shape[1], momentum_out.shape[1]
    return pl.pallas_call(
        functools.partial(finish_kernel, scale),
        name="finish_step",
        out_shape=(
            jax.ShapeDtypeStruct((count, width), BF),
            jax.ShapeDtypeStruct(momentum_in.shape, F32),
            jax.ShapeDtypeStruct(momentum_out.shape, F32),
        ),
        in_specs=[VMEM_SPEC] * 4,
        out_specs=(VMEM_SPEC,) * 3,
        scratch_shapes=[pltpu.VMEM((count, 128), jnp.int32), pltpu.VMEM((count, width), BF)],
        compiler_params=pltpu.CompilerParams(vmem_limit_bytes=32 << 20),
        cost_estimate=pl.CostEstimate(
            flops=2 * count * count * width, bytes_accessed=4 * count * width, transcendentals=0
        ),
    )(slots, arrived, momentum_in, momentum_out)


def layer(lens, dest, inbox, weights, upstream):
    count, width = inbox.shape
    tiles, pairs = count // TILE, width // 128
    kept = TILE * tiles * (tiles + 1) // 2
    return pl.pallas_call(
        layer_kernel,
        name="layer_step",
        out_shape=(
            jax.ShapeDtypeStruct((count, 4 * width), BF),
            jax.ShapeDtypeStruct((width, weights.shape[1] // 2), BF),
            jax.ShapeDtypeStruct((width, weights.shape[1] // 2), BF),
        ),
        in_specs=[SMEM_SPEC] + [VMEM_SPEC] * 4,
        out_specs=(VMEM_SPEC,) * 3,
        scratch_shapes=[
            pltpu.VMEM((count, 128), jnp.int32),
            pltpu.VMEM((width, count), BF),
            pltpu.VMEM((count, width), F32),
            pltpu.VMEM((count, width), BF),
            pltpu.VMEM((count, width), BF),
            pltpu.VMEM((count, width), BF),
            pltpu.VMEM((count, width), F32),
            pltpu.VMEM((width, count), BF),
            pltpu.VMEM((count, width), BF),
            pltpu.VMEM((pairs, 2 * TILE, kept), BF),
            pltpu.VMEM((pairs, 2 * TILE, kept), BF),
            pltpu.VMEM((128, count), F32),
            pltpu.VMEM((128, count), F32),
        ],
        compiler_params=pltpu.CompilerParams(vmem_limit_bytes=37 << 20),
        cost_estimate=pl.CostEstimate(
            flops=30_000_000_000, bytes_accessed=12_000_000, transcendentals=10_000_000
        ),
    )(lens, dest, inbox, weights, upstream)


def shards(events, home_slot, dest_slot, seq_lens, weights, out_grad, momentum_in, momentum_out):
    row_count, model_width = events.shape
    home = home_slot.reshape(1, row_count)
    dest = dest_slot.reshape(1, row_count)
    peers = lax.axis_size(DP)
    slots = row_count // peers

    def exchange(blocks):
        return lax.all_to_all(blocks, DP, split_axis=0, concat_axis=0, tiled=True)

    outbox = place(home, events).reshape(peers, slots, model_width)
    inbox = exchange(outbox).reshape(row_count, model_width)
    hidden_grad, kept, given = layer(seq_lens, dest, inbox, weights, out_grad)
    got = lax.ppermute(given, CORE, [(0, 1), (1, 0)])
    sendback = back(dest, hidden_grad, weights, out_grad)
    wire = pack(sendback.reshape(peers, slots, model_width), kept, got)
    grad_scale = (peers * row_count) ** (-0.5)
    return finish(grad_scale, home, exchange(wire), momentum_in, momentum_out)


def solution(mesh):
    split = Mesh(mesh.devices.reshape(4, 4, 4, 2), DP)
    return jax.shard_map(
        shards,
        mesh=split,
        in_specs=(P(DP, None), P(DP), P(DP), P(DP), P(), P(DP, None), P(DP, None), P(DP, None)),
        out_specs=(P(DP, None), P(DP, None), P(DP, None)),
        check_vma=False,
    )
```

```python
import functools

import jax
import jax.numpy as jnp
from jax import lax
from jax.experimental import pallas as pl
from jax.experimental.pallas import tpu as pltpu
from jax.sharding import Mesh
from jax.sharding import PartitionSpec as P

BLK = 512
DP = ("dp_0", "dp_1", "dp_2", "dp_3")
CHIPS = DP[:3]
CORE = DP[3]

NORM_EPS = 1e-05
DECAY = 0.9
TILE = 256
WIDE = 512
BF = jnp.bfloat16
F32 = jnp.float32


def dot(a, b):
    return jnp.dot(a, b, preferred_element_type=F32)


def dot_nt(a, b):
    return lax.dot_general(a, b, (((1,), (1,)), ((), ())), preferred_element_type=F32)


def dot_tn(a, b):
    return lax.dot_general(a, b, (((0,), (0,)), ((), ())), preferred_element_type=F32)


def rows_at(i, size=TILE):
    return pl.ds(pl.multiple_of(i * size, size), size)


def slot_rows(slots, first, count):
    places = lax.broadcasted_iota(jnp.int32, (count, slots.shape[1]), 0) + first
    return jnp.where(slots == places, 1.0, 0.0).astype(BF)


def slot_columns(spread, count, height=1.0):
    lane = lax.broadcasted_iota(jnp.int32, spread.shape, 1)
    parts = [
        jnp.where(spread == lane + at, height, 0.0).astype(BF) for at in range(0, count, 128)
    ]
    return jnp.concatenate(parts, axis=1)


def spread_slots(slots):
    return jnp.transpose(jnp.broadcast_to(slots, (128, slots.shape[1])))


def place_kernel(slots_ref, rows_ref, out_ref):
    @pl.loop(0, out_ref.shape[0] // WIDE)
    def _(i):
        pick = slot_rows(slots_ref[...], i * WIDE, WIDE)
        out_ref[rows_at(i, WIDE), :] = dot(pick, rows_ref[...]).astype(BF)


def silu_parts(half):
    plus = 1.0 + jnp.tanh(half)
    value = half * plus
    return value, plus + value * (2.0 - plus)


def two_heads(rows):
    lane = lax.broadcasted_iota(jnp.int32, rows.shape, 1)
    none = jnp.zeros_like(rows)
    low = lane < 64
    return jnp.concatenate([jnp.where(low, rows, none), jnp.where(low, none, rows)], axis=0)


def own_lanes(stacked):
    half = stacked.shape[0] // 2
    lane = lax.broadcasted_iota(jnp.int32, (half, stacked.shape[1]), 1)
    return jnp.where(lane < 64, stacked[:half], stacked[half:])


def layer_kernel(
    lens_ref,
    dest_ref,
    inbox_ref,
    weights_ref,
    upstream_ref,
    hidden_grad,
    kept_ref,
    given_ref,
    spread_ref,
    tokens_t,
    gate,
    vals,
    queries,
    keys,
    attended,
    mixed_t,
    att_grad,
    weights_kept,
    slopes_kept,
    key_sum,
    val_sum,
):
    row_count, width = inbox_ref.shape
    tiles = row_count // TILE
    pairs = width // 128
    first, second = lens_ref[0], lens_ref[1]
    joined = jnp.where(first > 0, first, second) > BLK
    spread_ref[...] = spread_slots(dest_ref[...])

    @pl.loop(0, row_count // WIDE)
    def _(i):
        rows = rows_at(i, WIDE)
        pick = slot_columns(spread_ref[rows, :], row_count, 0.5)
        tokens = dot(pick, inbox_ref[...]).astype(BF)
        tokens_t[:, rows] = tokens.T
        for g in range(4):
            columns = slice(g * width, (g + 1) * width)
            value, slope2 = silu_parts(dot(tokens, weights_ref[:, columns]))
            hidden_grad[rows, columns] = slope2.astype(BF)
            if g == 0:
                gate[rows, :] = value
            elif g == 1:
                vals[rows, :] = value.astype(BF)
            elif g == 2:
                queries[rows, :] = value.astype(BF) * jnp.asarray(0.0625, BF)
            else:
                keys[rows, :] = value.astype(BF)

    offsets = [sum(TILE * (t + 1) for t in range(i)) for i in range(tiles)]

    def forward_tile(p, i, low, high, edge):
        lanes = pl.ds(pl.multiple_of(p * 128, 128), 128)
        rows = slice(i * TILE, (i + 1) * TILE)
        kept = slice(offsets[i] + low, offsets[i] + high)
        stacked = two_heads(queries[rows, lanes])
        half = dot_nt(stacked, keys[low:high, lanes])
        plus = 1.0 + jnp.tanh(half)
        if edge:
            place = lax.broadcasted_iota(jnp.int32, (TILE, TILE), 0)
            seen = lax.broadcasted_iota(jnp.int32, (TILE, TILE), 1) <= place
            seen = jnp.concatenate([seen, seen], axis=0)
            cut = high - low - TILE
            last = jnp.where(seen, plus[:, cut:], 0.0)
            plus = jnp.concatenate([plus[:, :cut], last], axis=1) if cut else last
        weight = (half * plus).astype(BF)
        plus = plus.astype(BF)
        slope2 = plus + weight * (2.0 - plus)
        weights_kept[p, :, kept] = weight
        slopes_kept[p, :, kept] = slope2
        return rows, lanes, own_lanes(dot(weight, vals[low:high, lanes]))

    @pl.loop(0, pairs)
    def _(p):
        for i in range(tiles):
            rows, lanes, part = forward_tile(p, i, i * TILE // BLK * BLK, (i + 1) * TILE, True)
            attended[rows, lanes] = part

    @pl.when(joined)
    def _():
        @pl.loop(0, pairs)
        def _(p):
            for i in range(BLK // TILE, tiles):
                rows, lanes, part = forward_tile(p, i, 0, BLK, False)
                attended[rows, lanes] += part

    def backward_pair(p, reach):
        start = pl.multiple_of(p * 128, 128)
        lanes = pl.ds(start, 128)
        key_sum[...] = jnp.zeros_like(key_sum)
        val_sum[...] = jnp.zeros_like(val_sum)
        for i in range(tiles):
            rows = slice(i * TILE, (i + 1) * TILE)
            stacked = two_heads(queries[rows, lanes])
            down = two_heads(att_grad[rows, lanes])
            low, high = (0 if reach else (i * TILE) // BLK * BLK), (i + 1) * TILE
            kept = slice(offsets[i] + low, offsets[i] + high)
            score = dot_nt(down, vals[low:high, lanes]).astype(BF) * slopes_kept[p, :, kept]
            val_sum[:, low:high] += dot(down.T, weights_kept[p, :, kept])
            key_sum[:, low:high] += dot(stacked.T, score)
            attended[rows, :128] = own_lanes(dot(score, keys[low:high, lanes]))
        for source, group, factor in (
            (val_sum[...].T, 1, 1.0),
            (attended[:, :128], 2, 0.0625),
            (key_sum[...].T, 3, 1.0),
        ):
            columns = pl.ds(pl.multiple_of(start + group * width, 128), 128)
            rounded = (source * factor).astype(BF).astype(F32)
            hidden_grad[:, columns] = (rounded * hidden_grad[:, columns].astype(F32)).astype(BF)

    def over_pairs(step):
        @pl.when(joined)
        def _():
            pl.loop(0, pairs)(lambda p: step(p, True))

        @pl.when(jnp.logical_not(joined))
        def _():
            pl.loop(0, pairs)(lambda p: step(p, False))

    @pl.loop(0, tiles)
    def _(i):
        rows = rows_at(i)
        value = attended[rows, :]
        centre = jnp.mean(value, axis=1, keepdims=True)
        centred = value - centre
        spread = jnp.mean(centred * centred, axis=1, keepdims=True)
        scale = lax.rsqrt(spread + NORM_EPS)
        normed = centred * scale
        gates = gate[rows, :]
        mixed_t[:, rows] = (normed * gates).astype(BF).T
        mixed_grad = dot_nt(upstream_ref[rows, :], weights_ref[:, 4 * width :])
        hidden_grad[rows, :width] = (mixed_grad * normed * hidden_grad[rows, :width].astype(F32)).astype(BF)
        down = mixed_grad * gates
        mean_down = jnp.mean(down, axis=1, keepdims=True)
        mean_both = jnp.mean(down * normed, axis=1, keepdims=True)
        att_grad[rows, :] = (scale * (down - mean_down - normed * mean_both)).astype(BF)

    over_pairs(backward_pair)

    ours = lax.axis_index(CORE)
    halves = kept_ref.shape[1] // TILE
    inner = 4 * width // TILE - halves

    def write_half(half, ref):
        @pl.loop(0, inner if half else halves)
        def _(i):
            columns = hidden_grad[:, rows_at(i + half * halves)]
            ref[:, rows_at(i)] = dot(tokens_t[...], columns).astype(BF)

        if half:
            ref[:, inner * TILE :] = dot(mixed_t[...], upstream_ref[...]).astype(BF)

    for core in range(2):

        @pl.when(ours == core)
        def _(core=core):
            write_half(core, kept_ref)
            write_half(1 - core, given_ref)


def back_kernel(dest_ref, hidden_grad, weights_ref, upstream_ref, sendback_ref, token_grad):
    row_count, width = upstream_ref.shape

    @pl.loop(0, row_count // WIDE)
    def _(i):
        rows = rows_at(i, WIDE)
        total = dot_nt(hidden_grad[rows, :], weights_ref[:, : 4 * width])
        token_grad[rows, :] = (upstream_ref[rows, :].astype(F32) + 0.5 * total).astype(BF)

    @pl.loop(0, row_count // WIDE)
    def _(i):
        pick = slot_rows(dest_ref[...], i * WIDE, WIDE)
        sendback_ref[rows_at(i, WIDE), :] = dot(pick, token_grad[...]).astype(BF)


def pack_kernel(rows_ref, kept_ref, got_ref, out_ref):
    peers, slots, width = rows_ref.shape
    half = kept_ref.shape[1] // 2
    out_ref[:, :, :width] = rows_ref[...]
    both = (kept_ref[...].astype(F32) + got_ref[...].astype(F32)).reshape(peers // 2, 8, 2 * half)
    turned = pltpu.roll(both, 4, 1)
    upper = lax.broadcasted_iota(jnp.int32, (peers // 2, 8, half), 1) < 4
    even = jnp.where(upper, both[:, :, :half], turned[:, :, half:])
    odd = jnp.where(upper, turned[:, :, :half], both[:, :, half:])
    joint = jnp.stack([even, odd], axis=1).reshape(peers, 8, half)
    out_ref[:, :, width:] = joint.astype(BF)


def finish_kernel(scale, slots_ref, arrived_ref, in_ref, out_ref, events_ref, new_in, new_out, spread_ref, rows_ref):
    peers, slots, _ = arrived_ref.shape
    count, width = events_ref.shape
    spread_ref[...] = spread_slots(slots_ref[...])
    rows_ref[...] = arrived_ref[:, :, :width].reshape(count, width)

    @pl.loop(0, count // WIDE)
    def _(i):
        rows = rows_at(i, WIDE)
        pick = slot_columns(spread_ref[rows, :], count)
        events_ref[rows, :] = dot(pick, rows_ref[...]).astype(BF)

    part = arrived_ref.shape[2] - width

    def add(i, sums):
        return tuple(
            total + arrived_ref[2 * i + core, :, width:].astype(F32) for core, total in enumerate(sums)
        )

    none = jnp.zeros((slots, part), F32)
    sums = lax.fori_loop(0, peers // 2, add, (none, none))
    pieces = [total[4 * h : 4 * h + 4] for total in sums for h in range(2)]
    total = jnp.concatenate(pieces, axis=1) * scale
    inner = in_ref.shape[1]
    new_in[...] = DECAY * in_ref[...] + total[:, :inner]
    new_out[...] = DECAY * out_ref[...] + total[:, inner:]


VMEM_SPEC = pl.BlockSpec(memory_space=pltpu.VMEM)
SMEM_SPEC = pl.BlockSpec(memory_space=pltpu.SMEM)


def place(slots, rows):
    count, width = rows.shape
    return pl.pallas_call(
        place_kernel,
        name="place_rows",
        out_shape=jax.ShapeDtypeStruct((count, width), BF),
        in_specs=[VMEM_SPEC] * 2,
        out_specs=VMEM_SPEC,
        compiler_params=pltpu.CompilerParams(vmem_limit_bytes=12 << 20),
        cost_estimate=pl.CostEstimate(
            flops=2 * count * count * width, bytes_accessed=4 * count * width, transcendentals=0
        ),
    )(slots, rows)


def back(dest, hidden_grad, weights, upstream):
    count, width = upstream.shape
    return pl.pallas_call(
        back_kernel,
        name="back_rows",
        out_shape=jax.ShapeDtypeStruct((count, width), BF),
        in_specs=[VMEM_SPEC] * 4,
        out_specs=VMEM_SPEC,
        scratch_shapes=[pltpu.VMEM((count, width), BF)],
        compiler_params=pltpu.CompilerParams(vmem_limit_bytes=20 << 20),
        cost_estimate=pl.CostEstimate(
            flops=10 * count * width * width, bytes_accessed=10_000_000, transcendentals=0
        ),
    )(dest, hidden_grad, weights, upstream)


def pack(rows, kept, got):
    peers, slots, width = rows.shape
    out = (peers, slots, width + kept.shape[1] // 2)
    return pl.pallas_call(
        pack_kernel,
        name="pack_rows",
        out_shape=jax.ShapeDtypeStruct(out, BF),
        in_specs=[VMEM_SPEC] * 3,
        out_specs=VMEM_SPEC,
        compiler_params=pltpu.CompilerParams(vmem_limit_bytes=32 << 20),
        cost_estimate=pl.CostEstimate(
            flops=kept.size, bytes_accessed=2 * 2 * (rows.size + kept.size), transcendentals=0
        ),
    )(rows, kept, got)


def finish(scale, slots, arrived, momentum_in, momentum_out):
    count, width = slots.shape[1], momentum_out.shape[1]
    return pl.pallas_call(
        functools.partial(finish_kernel, scale),
        name="finish_step",
        out_shape=(
            jax.ShapeDtypeStruct((count, width), BF),
            jax.ShapeDtypeStruct(momentum_in.shape, F32),
            jax.ShapeDtypeStruct(momentum_out.shape, F32),
        ),
        in_specs=[VMEM_SPEC] * 4,
        out_specs=(VMEM_SPEC,) * 3,
        scratch_shapes=[pltpu.VMEM((count, 128), jnp.int32), pltpu.VMEM((count, width), BF)],
        compiler_params=pltpu.CompilerParams(vmem_limit_bytes=32 << 20),
        cost_estimate=pl.CostEstimate(
            flops=2 * count * count * width, bytes_accessed=4 * count * width, transcendentals=0
        ),
    )(slots, arrived, momentum_in, momentum_out)


def layer(lens, dest, inbox, weights, upstream):
    count, width = inbox.shape
    tiles, pairs = count // TILE, width // 128
    kept = TILE * tiles * (tiles + 1) // 2
    return pl.pallas_call(
        layer_kernel,
        name="layer_step",
        out_shape=(
            jax.ShapeDtypeStruct((count, 4 * width), BF),
            jax.ShapeDtypeStruct((width, weights.shape[1] // 2), BF),
            jax.ShapeDtypeStruct((width, weights.shape[1] // 2), BF),
        ),
        in_specs=[SMEM_SPEC] + [VMEM_SPEC] * 4,
        out_specs=(VMEM_SPEC,) * 3,
        scratch_shapes=[
            pltpu.VMEM((count, 128), jnp.int32),
            pltpu.VMEM((width, count), BF),
            pltpu.VMEM((count, width), F32),
            pltpu.VMEM((count, width), BF),
            pltpu.VMEM((count, width), BF),
            pltpu.VMEM((count, width), BF),
            pltpu.VMEM((count, width), F32),
            pltpu.VMEM((width, count), BF),
            pltpu.VMEM((count, width), BF),
            pltpu.VMEM((pairs, 2 * TILE, kept), BF),
            pltpu.VMEM((pairs, 2 * TILE, kept), BF),
            pltpu.VMEM((128, count), F32),
            pltpu.VMEM((128, count), F32),
        ],
        compiler_params=pltpu.CompilerParams(vmem_limit_bytes=37 << 20),
        cost_estimate=pl.CostEstimate(
            flops=30_000_000_000, bytes_accessed=12_000_000, transcendentals=10_000_000
        ),
    )(lens, dest, inbox, weights, upstream)


def shards(events, home_slot, dest_slot, seq_lens, weights, out_grad, momentum_in, momentum_out):
    row_count, model_width = events.shape
    home = home_slot.reshape(1, row_count)
    dest = dest_slot.reshape(1, row_count)
    peers = lax.axis_size(DP)
    slots = row_count // peers

    def exchange(blocks):
        return lax.all_to_all(blocks, DP, split_axis=0, concat_axis=0, tiled=True)

    outbox = place(home, events).reshape(peers, slots, model_width)
    inbox = exchange(outbox).reshape(row_count, model_width)
    hidden_grad, kept, given = layer(seq_lens, dest, inbox, weights, out_grad)
    got = lax.ppermute(given, CORE, [(0, 1), (1, 0)])
    sendback = back(dest, hidden_grad, weights, out_grad)
    wire = pack(sendback.reshape(peers, slots, model_width), kept, got)
    grad_scale = (peers * row_count) ** (-0.5)
    return finish(grad_scale, home, exchange(wire), momentum_in, momentum_out)


def solution(mesh):
    split = Mesh(mesh.devices.reshape(4, 4, 4, 2), DP)
    return jax.shard_map(
        shards,
        mesh=split,
        in_specs=(P(DP, None), P(DP), P(DP), P(DP), P(), P(DP, None), P(DP, None), P(DP, None)),
        out_specs=(P(DP, None), P(DP, None), P(DP, None)),
        check_vma=False,
    )
```

```python
import functools

import jax
import jax.numpy as jnp
from jax import lax
from jax.experimental import pallas as pl
from jax.experimental.pallas import tpu as pltpu
from jax.sharding import Mesh
from jax.sharding import PartitionSpec as P

BLK = 512
DP = ("dp_0", "dp_1", "dp_2", "dp_3")
CHIPS = DP[:3]
CORE = DP[3]

NORM_EPS = 1e-05
DECAY = 0.9
TILE = 256
WIDE = 512
BF = jnp.bfloat16
F32 = jnp.float32


def dot(a, b):
    return jnp.dot(a, b, preferred_element_type=F32)


def dot_nt(a, b):
    return lax.dot_general(a, b, (((1,), (1,)), ((), ())), preferred_element_type=F32)


def dot_tn(a, b):
    return lax.dot_general(a, b, (((0,), (0,)), ((), ())), preferred_element_type=F32)


def rows_at(i, size=TILE):
    return pl.ds(pl.multiple_of(i * size, size), size)


def slot_rows(slots, first, count):
    places = lax.broadcasted_iota(jnp.int32, (count, slots.shape[1]), 0) + first
    return jnp.where(slots == places, 1.0, 0.0).astype(BF)


def slot_columns(spread, count, height=1.0):
    lane = lax.broadcasted_iota(jnp.int32, spread.shape, 1)
    parts = [
        jnp.where(spread == lane + at, height, 0.0).astype(BF) for at in range(0, count, 128)
    ]
    return jnp.concatenate(parts, axis=1)


def spread_slots(slots):
    return jnp.transpose(jnp.broadcast_to(slots, (128, slots.shape[1])))


def place_kernel(slots_ref, rows_ref, out_ref):
    @pl.loop(0, out_ref.shape[0] // WIDE)
    def _(i):
        pick = slot_rows(slots_ref[...], i * WIDE, WIDE)
        out_ref[rows_at(i, WIDE), :] = dot(pick, rows_ref[...]).astype(BF)


def silu_parts(half):
    plus = 1.0 + jnp.tanh(half)
    value = half * plus
    return value, plus + value * (2.0 - plus)


def two_heads(rows):
    lane = lax.broadcasted_iota(jnp.int32, rows.shape, 1)
    none = jnp.zeros_like(rows)
    low = lane < 64
    return jnp.concatenate([jnp.where(low, rows, none), jnp.where(low, none, rows)], axis=0)


def own_lanes(stacked):
    half = stacked.shape[0] // 2
    lane = lax.broadcasted_iota(jnp.int32, (half, stacked.shape[1]), 1)
    return jnp.where(lane < 64, stacked[:half], stacked[half:])


def layer_kernel(
    lens_ref,
    dest_ref,
    inbox_ref,
    weights_ref,
    upstream_ref,
    hidden_grad,
    kept_ref,
    given_ref,
    spread_ref,
    tokens_t,
    gate,
    vals,
    queries,
    keys,
    attended,
    mixed_t,
    att_grad,
    weights_kept,
    slopes_kept,
    key_sum,
    val_sum,
):
    row_count, width = inbox_ref.shape
    tiles = row_count // TILE
    pairs = width // 128
    first, second = lens_ref[0], lens_ref[1]
    joined = jnp.where(first > 0, first, second) > BLK
    spread_ref[...] = spread_slots(dest_ref[...])

    @pl.loop(0, row_count // WIDE)
    def _(i):
        rows = rows_at(i, WIDE)
        pick = slot_columns(spread_ref[rows, :], row_count, 0.5)
        tokens = dot(pick, inbox_ref[...]).astype(BF)
        tokens_t[:, rows] = tokens.T
        for g in range(4):
            columns = slice(g * width, (g + 1) * width)
            value, slope2 = silu_parts(dot(tokens, weights_ref[:, columns]))
            hidden_grad[rows, columns] = slope2.astype(BF)
            if g == 0:
                gate[rows, :] = value
            elif g == 1:
                vals[rows, :] = value.astype(BF)
            elif g == 2:
                queries[rows, :] = value.astype(BF) * jnp.asarray(0.0625, BF)
            else:
                keys[rows, :] = value.astype(BF)

    offsets = [sum(TILE * (t + 1) for t in range(i)) for i in range(tiles)]

    def forward_tile(p, i, low, high, edge):
        lanes = pl.ds(pl.multiple_of(p * 128, 128), 128)
        rows = slice(i * TILE, (i + 1) * TILE)
        kept = slice(offsets[i] + low, offsets[i] + high)
        stacked = two_heads(queries[rows, lanes])
        half = dot_nt(stacked, keys[low:high, lanes])
        plus = 1.0 + jnp.tanh(half)
        if edge:
            place = lax.broadcasted_iota(jnp.int32, (TILE, TILE), 0)
            seen = lax.broadcasted_iota(jnp.int32, (TILE, TILE), 1) <= place
            seen = jnp.concatenate([seen, seen], axis=0)
            cut = high - low - TILE
            last = jnp.where(seen, plus[:, cut:], 0.0)
            plus = jnp.concatenate([plus[:, :cut], last], axis=1) if cut else last
        weight = (half * plus).astype(BF)
        plus = plus.astype(BF)
        slope2 = plus + weight * (2.0 - plus)
        weights_kept[p, :, kept] = weight
        slopes_kept[p, :, kept] = slope2
        return rows, lanes, own_lanes(dot(weight, vals[low:high, lanes]))

    def forward_pair(p, reach):
        for i in range(tiles):
            low = i * TILE // BLK * BLK
            rows, lanes, part = forward_tile(p, i, low, (i + 1) * TILE, True)
            if reach and low > 0:
                part += forward_tile(p, i, 0, low, False)[2]
            attended[rows, lanes] = part

    def backward_pair(p, reach):
        start = pl.multiple_of(p * 128, 128)
        lanes = pl.ds(start, 128)
        key_sum[...] = jnp.zeros_like(key_sum)
        val_sum[...] = jnp.zeros_like(val_sum)
        for i in range(tiles):
            rows = slice(i * TILE, (i + 1) * TILE)
            stacked = two_heads(queries[rows, lanes])
            down = two_heads(att_grad[rows, lanes])
            low, high = (0 if reach else (i * TILE) // BLK * BLK), (i + 1) * TILE
            kept = slice(offsets[i] + low, offsets[i] + high)
            score = dot_nt(down, vals[low:high, lanes]).astype(BF) * slopes_kept[p, :, kept]
            val_sum[:, low:high] += dot(down.T, weights_kept[p, :, kept])
            key_sum[:, low:high] += dot(stacked.T, score)
            attended[rows, :128] = own_lanes(dot(score, keys[low:high, lanes]))
        for source, group, factor in (
            (val_sum[...].T, 1, 1.0),
            (attended[:, :128], 2, 0.0625),
            (key_sum[...].T, 3, 1.0),
        ):
            columns = pl.ds(pl.multiple_of(start + group * width, 128), 128)
            rounded = (source * factor).astype(BF).astype(F32)
            hidden_grad[:, columns] = (rounded * hidden_grad[:, columns].astype(F32)).astype(BF)

    def over_pairs(step):
        @pl.when(joined)
        def _():
            pl.loop(0, pairs)(lambda p: step(p, True))

        @pl.when(jnp.logical_not(joined))
        def _():
            pl.loop(0, pairs)(lambda p: step(p, False))

    over_pairs(forward_pair)

    @pl.loop(0, tiles)
    def _(i):
        rows = rows_at(i)
        value = attended[rows, :]
        centre = jnp.mean(value, axis=1, keepdims=True)
        centred = value - centre
        spread = jnp.mean(centred * centred, axis=1, keepdims=True)
        scale = lax.rsqrt(spread + NORM_EPS)
        normed = centred * scale
        gates = gate[rows, :]
        mixed_t[:, rows] = (normed * gates).astype(BF).T
        mixed_grad = dot_nt(upstream_ref[rows, :], weights_ref[:, 4 * width :])
        hidden_grad[rows, :width] = (mixed_grad * normed * hidden_grad[rows, :width].astype(F32)).astype(BF)
        down = mixed_grad * gates
        mean_down = jnp.mean(down, axis=1, keepdims=True)
        mean_both = jnp.mean(down * normed, axis=1, keepdims=True)
        att_grad[rows, :] = (scale * (down - mean_down - normed * mean_both)).astype(BF)

    over_pairs(backward_pair)

    ours = lax.axis_index(CORE)
    halves = kept_ref.shape[1] // TILE
    inner = 4 * width // TILE - halves

    def write_half(half, ref):
        @pl.loop(0, inner if half else halves)
        def _(i):
            columns = hidden_grad[:, rows_at(i + half * halves)]
            ref[:, rows_at(i)] = dot(tokens_t[...], columns).astype(BF)

        if half:
            ref[:, inner * TILE :] = dot(mixed_t[...], upstream_ref[...]).astype(BF)

    for core in range(2):

        @pl.when(ours == core)
        def _(core=core):
            write_half(core, kept_ref)
            write_half(1 - core, given_ref)


def back_kernel(dest_ref, hidden_grad, weights_ref, upstream_ref, sendback_ref, token_grad):
    row_count, width = upstream_ref.shape

    @pl.loop(0, row_count // WIDE)
    def _(i):
        rows = rows_at(i, WIDE)
        total = dot_nt(hidden_grad[rows, :], weights_ref[:, : 4 * width])
        token_grad[rows, :] = (upstream_ref[rows, :].astype(F32) + 0.5 * total).astype(BF)

    @pl.loop(0, row_count // WIDE)
    def _(i):
        pick = slot_rows(dest_ref[...], i * WIDE, WIDE)
        sendback_ref[rows_at(i, WIDE), :] = dot(pick, token_grad[...]).astype(BF)


def pack_kernel(rows_ref, kept_ref, got_ref, out_ref):
    peers, slots, width = rows_ref.shape
    half = kept_ref.shape[1] // 2
    out_ref[:, :, :width] = rows_ref[...]
    both = (kept_ref[...].astype(F32) + got_ref[...].astype(F32)).reshape(peers // 2, 8, 2 * half)
    turned = pltpu.roll(both, 4, 1)
    upper = lax.broadcasted_iota(jnp.int32, (peers // 2, 8, half), 1) < 4
    even = jnp.where(upper, both[:, :, :half], turned[:, :, half:])
    odd = jnp.where(upper, turned[:, :, :half], both[:, :, half:])
    joint = jnp.stack([even, odd], axis=1).reshape(peers, 8, half)
    out_ref[:, :, width:] = joint.astype(BF)


def finish_kernel(scale, slots_ref, arrived_ref, in_ref, out_ref, events_ref, new_in, new_out, spread_ref, rows_ref):
    peers, slots, _ = arrived_ref.shape
    count, width = events_ref.shape
    spread_ref[...] = spread_slots(slots_ref[...])
    rows_ref[...] = arrived_ref[:, :, :width].reshape(count, width)

    @pl.loop(0, count // WIDE)
    def _(i):
        rows = rows_at(i, WIDE)
        pick = slot_columns(spread_ref[rows, :], count)
        events_ref[rows, :] = dot(pick, rows_ref[...]).astype(BF)

    part = arrived_ref.shape[2] - width

    def add(i, sums):
        return tuple(
            total + arrived_ref[2 * i + core, :, width:].astype(F32) for core, total in enumerate(sums)
        )

    none = jnp.zeros((slots, part), F32)
    sums = lax.fori_loop(0, peers // 2, add, (none, none))
    pieces = [total[4 * h : 4 * h + 4] for total in sums for h in range(2)]
    total = jnp.concatenate(pieces, axis=1) * scale
    inner = in_ref.shape[1]
    new_in[...] = DECAY * in_ref[...] + total[:, :inner]
    new_out[...] = DECAY * out_ref[...] + total[:, inner:]


VMEM_SPEC = pl.BlockSpec(memory_space=pltpu.VMEM)
SMEM_SPEC = pl.BlockSpec(memory_space=pltpu.SMEM)


def place(slots, rows):
    count, width = rows.shape
    return pl.pallas_call(
        place_kernel,
        name="place_rows",
        out_shape=jax.ShapeDtypeStruct((count, width), BF),
        in_specs=[VMEM_SPEC] * 2,
        out_specs=VMEM_SPEC,
        compiler_params=pltpu.CompilerParams(vmem_limit_bytes=12 << 20),
        cost_estimate=pl.CostEstimate(
            flops=2 * count * count * width, bytes_accessed=4 * count * width, transcendentals=0
        ),
    )(slots, rows)


def back(dest, hidden_grad, weights, upstream):
    count, width = upstream.shape
    return pl.pallas_call(
        back_kernel,
        name="back_rows",
        out_shape=jax.ShapeDtypeStruct((count, width), BF),
        in_specs=[VMEM_SPEC] * 4,
        out_specs=VMEM_SPEC,
        scratch_shapes=[pltpu.VMEM((count, width), BF)],
        compiler_params=pltpu.CompilerParams(vmem_limit_bytes=20 << 20),
        cost_estimate=pl.CostEstimate(
            flops=10 * count * width * width, bytes_accessed=10_000_000, transcendentals=0
        ),
    )(dest, hidden_grad, weights, upstream)


def pack(rows, kept, got):
    peers, slots, width = rows.shape
    out = (peers, slots, width + kept.shape[1] // 2)
    return pl.pallas_call(
        pack_kernel,
        name="pack_rows",
        out_shape=jax.ShapeDtypeStruct(out, BF),
        in_specs=[VMEM_SPEC] * 3,
        out_specs=VMEM_SPEC,
        compiler_params=pltpu.CompilerParams(vmem_limit_bytes=32 << 20),
        cost_estimate=pl.CostEstimate(
            flops=kept.size, bytes_accessed=2 * 2 * (rows.size + kept.size), transcendentals=0
        ),
    )(rows, kept, got)


def finish(scale, slots, arrived, momentum_in, momentum_out):
    count, width = slots.shape[1], momentum_out.shape[1]
    return pl.pallas_call(
        functools.partial(finish_kernel, scale),
        name="finish_step",
        out_shape=(
            jax.ShapeDtypeStruct((count, width), BF),
            jax.ShapeDtypeStruct(momentum_in.shape, F32),
            jax.ShapeDtypeStruct(momentum_out.shape, F32),
        ),
        in_specs=[VMEM_SPEC] * 4,
        out_specs=(VMEM_SPEC,) * 3,
        scratch_shapes=[pltpu.VMEM((count, 128), jnp.int32), pltpu.VMEM((count, width), BF)],
        compiler_params=pltpu.CompilerParams(vmem_limit_bytes=32 << 20),
        cost_estimate=pl.CostEstimate(
            flops=2 * count * count * width, bytes_accessed=4 * count * width, transcendentals=0
        ),
    )(slots, arrived, momentum_in, momentum_out)


def layer(lens, dest, inbox, weights, upstream):
    count, width = inbox.shape
    tiles, pairs = count // TILE, width // 128
    kept = TILE * tiles * (tiles + 1) // 2
    return pl.pallas_call(
        layer_kernel,
        name="layer_step",
        out_shape=(
            jax.ShapeDtypeStruct((count, 4 * width), BF),
            jax.ShapeDtypeStruct((width, weights.shape[1] // 2), BF),
            jax.ShapeDtypeStruct((width, weights.shape[1] // 2), BF),
        ),
        in_specs=[SMEM_SPEC] + [VMEM_SPEC] * 4,
        out_specs=(VMEM_SPEC,) * 3,
        scratch_shapes=[
            pltpu.VMEM((count, 128), jnp.int32),
            pltpu.VMEM((width, count), BF),
            pltpu.VMEM((count, width), F32),
            pltpu.VMEM((count, width), BF),
            pltpu.VMEM((count, width), BF),
            pltpu.VMEM((count, width), BF),
            pltpu.VMEM((count, width), F32),
            pltpu.VMEM((width, count), BF),
            pltpu.VMEM((count, width), BF),
            pltpu.VMEM((pairs, 2 * TILE, kept), BF),
            pltpu.VMEM((pairs, 2 * TILE, kept), BF),
            pltpu.VMEM((128, count), F32),
            pltpu.VMEM((128, count), F32),
        ],
        compiler_params=pltpu.CompilerParams(vmem_limit_bytes=37 << 20),
        cost_estimate=pl.CostEstimate(
            flops=30_000_000_000, bytes_accessed=12_000_000, transcendentals=10_000_000
        ),
    )(lens, dest, inbox, weights, upstream)


def shards(events, home_slot, dest_slot, seq_lens, weights, out_grad, momentum_in, momentum_out):
    row_count, model_width = events.shape
    home = home_slot.reshape(1, row_count)
    dest = dest_slot.reshape(1, row_count)
    peers = lax.axis_size(DP)
    slots = row_count // peers

    def exchange(blocks):
        return lax.all_to_all(blocks, DP, split_axis=0, concat_axis=0, tiled=True)

    outbox = place(home, events).reshape(peers, slots, model_width)
    inbox = exchange(outbox).reshape(row_count, model_width)
    hidden_grad, kept, given = layer(seq_lens, dest, inbox, weights, out_grad)
    got = lax.ppermute(given, CORE, [(0, 1), (1, 0)])
    sendback = back(dest, hidden_grad, weights, out_grad)
    wire = pack(sendback.reshape(peers, slots, model_width), kept, got)
    grad_scale = (peers * row_count) ** (-0.5)
    return finish(grad_scale, home, exchange(wire), momentum_in, momentum_out)


def solution(mesh):
    split = Mesh(mesh.devices.reshape(4, 4, 4, 2), DP)
    return jax.shard_map(
        shards,
        mesh=split,
        in_specs=(P(DP, None), P(DP), P(DP), P(DP), P(), P(DP, None), P(DP, None), P(DP, None)),
        out_specs=(P(DP, None), P(DP, None), P(DP, None)),
        check_vma=False,
    )
```

```python
import functools

import jax
import jax.numpy as jnp
from jax import lax
from jax.experimental import pallas as pl
from jax.experimental.pallas import tpu as pltpu
from jax.sharding import Mesh
from jax.sharding import PartitionSpec as P

BLK = 512
DP = ("dp_0", "dp_1", "dp_2", "dp_3")
CHIPS = DP[:3]
CORE = DP[3]

NORM_EPS = 1e-05
DECAY = 0.9
TILE = 256
WIDE = 512
BF = jnp.bfloat16
F32 = jnp.float32


def dot(a, b):
    return jnp.dot(a, b, preferred_element_type=F32)


def dot_nt(a, b):
    return lax.dot_general(a, b, (((1,), (1,)), ((), ())), preferred_element_type=F32)


def dot_tn(a, b):
    return lax.dot_general(a, b, (((0,), (0,)), ((), ())), preferred_element_type=F32)


def rows_at(i, size=TILE):
    return pl.ds(pl.multiple_of(i * size, size), size)


def slot_rows(slots, first, count):
    places = lax.broadcasted_iota(jnp.int32, (count, slots.shape[1]), 0) + first
    return jnp.where(slots == places, 1.0, 0.0).astype(BF)


def slot_columns(spread, count, height=1.0):
    lane = lax.broadcasted_iota(jnp.int32, spread.shape, 1)
    parts = [
        jnp.where(spread == lane + at, height, 0.0).astype(BF) for at in range(0, count, 128)
    ]
    return jnp.concatenate(parts, axis=1)


def spread_slots(slots):
    return jnp.transpose(jnp.broadcast_to(slots, (128, slots.shape[1])))


def place_kernel(slots_ref, rows_ref, out_ref):
    @pl.loop(0, out_ref.shape[0] // WIDE)
    def _(i):
        pick = slot_rows(slots_ref[...], i * WIDE, WIDE)
        out_ref[rows_at(i, WIDE), :] = dot(pick, rows_ref[...]).astype(BF)


def silu_parts(half):
    plus = 1.0 + jnp.tanh(half)
    value = half * plus
    return value, plus + value * (2.0 - plus)


def two_heads(rows):
    lane = lax.broadcasted_iota(jnp.int32, rows.shape, 1)
    none = jnp.zeros_like(rows)
    low = lane < 64
    return jnp.concatenate([jnp.where(low, rows, none), jnp.where(low, none, rows)], axis=0)


def own_lanes(stacked):
    half = stacked.shape[0] // 2
    lane = lax.broadcasted_iota(jnp.int32, (half, stacked.shape[1]), 1)
    return jnp.where(lane < 64, stacked[:half], stacked[half:])


def layer_kernel(
    lens_ref,
    dest_ref,
    inbox_ref,
    weights_ref,
    upstream_ref,
    hidden_grad,
    kept_ref,
    given_ref,
    spread_ref,
    tokens_t,
    gate,
    vals,
    queries,
    keys,
    attended,
    mixed_t,
    att_grad,
    weights_kept,
    slopes_kept,
    key_sum,
    val_sum,
):
    row_count, width = inbox_ref.shape
    tiles = row_count // TILE
    pairs = width // 128
    first, second = lens_ref[0], lens_ref[1]
    joined = jnp.where(first > 0, first, second) > BLK
    spread_ref[...] = spread_slots(dest_ref[...])

    @pl.loop(0, row_count // WIDE)
    def _(i):
        rows = rows_at(i, WIDE)
        pick = slot_columns(spread_ref[rows, :], row_count, 0.5)
        tokens = dot(pick, inbox_ref[...]).astype(BF)
        tokens_t[:, rows] = tokens.T
        for g in range(4):
            columns = slice(g * width, (g + 1) * width)
            value, slope2 = silu_parts(dot(tokens, weights_ref[:, columns]))
            hidden_grad[rows, columns] = slope2.astype(BF)
            if g == 0:
                gate[rows, :] = value
            elif g == 1:
                vals[rows, :] = value.astype(BF)
            elif g == 2:
                queries[rows, :] = value.astype(BF) * jnp.asarray(0.0625, BF)
            else:
                keys[rows, :] = value.astype(BF)

    offsets = [sum(TILE * (t + 1) for t in range(i)) for i in range(tiles)]

    def forward_tile(p, i, low, high, edge):
        lanes = pl.ds(pl.multiple_of(p * 128, 128), 128)
        rows = slice(i * TILE, (i + 1) * TILE)
        kept = slice(offsets[i] + low, offsets[i] + high)
        stacked = two_heads(queries[rows, lanes])
        half = dot_nt(stacked, keys[low:high, lanes])
        plus = 1.0 + jnp.tanh(half)
        if edge:
            place = lax.broadcasted_iota(jnp.int32, (TILE, TILE), 0)
            seen = lax.broadcasted_iota(jnp.int32, (TILE, TILE), 1) <= place
            seen = jnp.concatenate([seen, seen], axis=0)
            cut = high - low - TILE
            last = jnp.where(seen, plus[:, cut:], 0.0)
            plus = jnp.concatenate([plus[:, :cut], last], axis=1) if cut else last
        weight = (half * plus).astype(BF)
        plus = plus.astype(BF)
        slope2 = plus + weight * (2.0 - plus)
        weights_kept[p, :, kept] = weight
        slopes_kept[p, :, kept] = slope2
        return rows, lanes, own_lanes(dot(weight, vals[low:high, lanes]))

    def forward_pair(p, reach):
        for i in range(tiles):
            low = i * TILE // BLK * BLK
            rows, lanes, part = forward_tile(p, i, low, (i + 1) * TILE, True)
            if reach and low > 0:
                part += forward_tile(p, i, 0, low, False)[2]
            attended[rows, lanes] = part

    def backward_pair(p, reach):
        start = pl.multiple_of(p * 128, 128)
        lanes = pl.ds(start, 128)
        key_sum[...] = jnp.zeros_like(key_sum)
        val_sum[...] = jnp.zeros_like(val_sum)
        for i in range(tiles):
            rows = slice(i * TILE, (i + 1) * TILE)
            stacked = two_heads(queries[rows, lanes])
            down = two_heads(att_grad[rows, lanes])
            low, high = (0 if reach else (i * TILE) // BLK * BLK), (i + 1) * TILE
            kept = slice(offsets[i] + low, offsets[i] + high)
            score = dot_nt(down, vals[low:high, lanes]).astype(BF) * slopes_kept[p, :, kept]
            val_sum[:, low:high] += dot(down.T, weights_kept[p, :, kept])
            key_sum[:, low:high] += dot(stacked.T, score)
            attended[rows, :128] = own_lanes(dot(score, keys[low:high, lanes]))
        for source, group, factor in (
            (val_sum[...].T, 1, 1.0),
            (attended[:, :128], 2, 0.0625),
            (key_sum[...].T, 3, 1.0),
        ):
            columns = pl.ds(pl.multiple_of(start + group * width, 128), 128)
            rounded = (source * factor).astype(BF).astype(F32)
            hidden_grad[:, columns] = (rounded * hidden_grad[:, columns].astype(F32)).astype(BF)

    def over_pairs(step, unroll):
        @pl.when(joined)
        def _():
            pl.loop(0, pairs, unroll=unroll)(lambda p: step(p, True))

        @pl.when(jnp.logical_not(joined))
        def _():
            pl.loop(0, pairs, unroll=unroll)(lambda p: step(p, False))

    over_pairs(forward_pair, 2)

    @pl.loop(0, tiles)
    def _(i):
        rows = rows_at(i)
        value = attended[rows, :]
        centre = jnp.mean(value, axis=1, keepdims=True)
        centred = value - centre
        spread = jnp.mean(centred * centred, axis=1, keepdims=True)
        scale = lax.rsqrt(spread + NORM_EPS)
        normed = centred * scale
        gates = gate[rows, :]
        mixed_t[:, rows] = (normed * gates).astype(BF).T
        mixed_grad = dot_nt(upstream_ref[rows, :], weights_ref[:, 4 * width :])
        hidden_grad[rows, :width] = (mixed_grad * normed * hidden_grad[rows, :width].astype(F32)).astype(BF)
        down = mixed_grad * gates
        mean_down = jnp.mean(down, axis=1, keepdims=True)
        mean_both = jnp.mean(down * normed, axis=1, keepdims=True)
        att_grad[rows, :] = (scale * (down - mean_down - normed * mean_both)).astype(BF)

    over_pairs(backward_pair, 1)

    ours = lax.axis_index(CORE)
    halves = kept_ref.shape[1] // TILE
    inner = 4 * width // TILE - halves

    def write_half(half, ref):
        @pl.loop(0, inner if half else halves)
        def _(i):
            columns = hidden_grad[:, rows_at(i + half * halves)]
            ref[:, rows_at(i)] = dot(tokens_t[...], columns).astype(BF)

        if half:
            ref[:, inner * TILE :] = dot(mixed_t[...], upstream_ref[...]).astype(BF)

    for core in range(2):

        @pl.when(ours == core)
        def _(core=core):
            write_half(core, kept_ref)
            write_half(1 - core, given_ref)


def back_kernel(dest_ref, hidden_grad, weights_ref, upstream_ref, sendback_ref, token_grad):
    row_count, width = upstream_ref.shape

    @pl.loop(0, row_count // WIDE)
    def _(i):
        rows = rows_at(i, WIDE)
        total = dot_nt(hidden_grad[rows, :], weights_ref[:, : 4 * width])
        token_grad[rows, :] = (upstream_ref[rows, :].astype(F32) + 0.5 * total).astype(BF)

    @pl.loop(0, row_count // WIDE)
    def _(i):
        pick = slot_rows(dest_ref[...], i * WIDE, WIDE)
        sendback_ref[rows_at(i, WIDE), :] = dot(pick, token_grad[...]).astype(BF)


def pack_kernel(rows_ref, kept_ref, got_ref, out_ref):
    peers, slots, width = rows_ref.shape
    half = kept_ref.shape[1] // 2
    out_ref[:, :, :width] = rows_ref[...]
    both = (kept_ref[...].astype(F32) + got_ref[...].astype(F32)).reshape(peers // 2, 8, 2 * half)
    turned = pltpu.roll(both, 4, 1)
    upper = lax.broadcasted_iota(jnp.int32, (peers // 2, 8, half), 1) < 4
    even = jnp.where(upper, both[:, :, :half], turned[:, :, half:])
    odd = jnp.where(upper, turned[:, :, :half], both[:, :, half:])
    joint = jnp.stack([even, odd], axis=1).reshape(peers, 8, half)
    out_ref[:, :, width:] = joint.astype(BF)


def finish_kernel(scale, slots_ref, arrived_ref, in_ref, out_ref, events_ref, new_in, new_out, spread_ref, rows_ref):
    peers, slots, _ = arrived_ref.shape
    count, width = events_ref.shape
    spread_ref[...] = spread_slots(slots_ref[...])
    rows_ref[...] = arrived_ref[:, :, :width].reshape(count, width)

    @pl.loop(0, count // WIDE)
    def _(i):
        rows = rows_at(i, WIDE)
        pick = slot_columns(spread_ref[rows, :], count)
        events_ref[rows, :] = dot(pick, rows_ref[...]).astype(BF)

    part = arrived_ref.shape[2] - width

    def add(i, sums):
        return tuple(
            total + arrived_ref[2 * i + core, :, width:].astype(F32) for core, total in enumerate(sums)
        )

    none = jnp.zeros((slots, part), F32)
    sums = lax.fori_loop(0, peers // 2, add, (none, none))
    pieces = [total[4 * h : 4 * h + 4] for total in sums for h in range(2)]
    total = jnp.concatenate(pieces, axis=1) * scale
    inner = in_ref.shape[1]
    new_in[...] = DECAY * in_ref[...] + total[:, :inner]
    new_out[...] = DECAY * out_ref[...] + total[:, inner:]


VMEM_SPEC = pl.BlockSpec(memory_space=pltpu.VMEM)
SMEM_SPEC = pl.BlockSpec(memory_space=pltpu.SMEM)


def place(slots, rows):
    count, width = rows.shape
    return pl.pallas_call(
        place_kernel,
        name="place_rows",
        out_shape=jax.ShapeDtypeStruct((count, width), BF),
        in_specs=[VMEM_SPEC] * 2,
        out_specs=VMEM_SPEC,
        compiler_params=pltpu.CompilerParams(vmem_limit_bytes=12 << 20),
        cost_estimate=pl.CostEstimate(
            flops=2 * count * count * width, bytes_accessed=4 * count * width, transcendentals=0
        ),
    )(slots, rows)


def back(dest, hidden_grad, weights, upstream):
    count, width = upstream.shape
    return pl.pallas_call(
        back_kernel,
        name="back_rows",
        out_shape=jax.ShapeDtypeStruct((count, width), BF),
        in_specs=[VMEM_SPEC] * 4,
        out_specs=VMEM_SPEC,
        scratch_shapes=[pltpu.VMEM((count, width), BF)],
        compiler_params=pltpu.CompilerParams(vmem_limit_bytes=20 << 20),
        cost_estimate=pl.CostEstimate(
            flops=10 * count * width * width, bytes_accessed=10_000_000, transcendentals=0
        ),
    )(dest, hidden_grad, weights, upstream)


def pack(rows, kept, got):
    peers, slots, width = rows.shape
    out = (peers, slots, width + kept.shape[1] // 2)
    return pl.pallas_call(
        pack_kernel,
        name="pack_rows",
        out_shape=jax.ShapeDtypeStruct(out, BF),
        in_specs=[VMEM_SPEC] * 3,
        out_specs=VMEM_SPEC,
        compiler_params=pltpu.CompilerParams(vmem_limit_bytes=32 << 20),
        cost_estimate=pl.CostEstimate(
            flops=kept.size, bytes_accessed=2 * 2 * (rows.size + kept.size), transcendentals=0
        ),
    )(rows, kept, got)


def finish(scale, slots, arrived, momentum_in, momentum_out):
    count, width = slots.shape[1], momentum_out.shape[1]
    return pl.pallas_call(
        functools.partial(finish_kernel, scale),
        name="finish_step",
        out_shape=(
            jax.ShapeDtypeStruct((count, width), BF),
            jax.ShapeDtypeStruct(momentum_in.shape, F32),
            jax.ShapeDtypeStruct(momentum_out.shape, F32),
        ),
        in_specs=[VMEM_SPEC] * 4,
        out_specs=(VMEM_SPEC,) * 3,
        scratch_shapes=[pltpu.VMEM((count, 128), jnp.int32), pltpu.VMEM((count, width), BF)],
        compiler_params=pltpu.CompilerParams(vmem_limit_bytes=32 << 20),
        cost_estimate=pl.CostEstimate(
            flops=2 * count * count * width, bytes_accessed=4 * count * width, transcendentals=0
        ),
    )(slots, arrived, momentum_in, momentum_out)


def layer(lens, dest, inbox, weights, upstream):
    count, width = inbox.shape
    tiles, pairs = count // TILE, width // 128
    kept = TILE * tiles * (tiles + 1) // 2
    return pl.pallas_call(
        layer_kernel,
        name="layer_step",
        out_shape=(
            jax.ShapeDtypeStruct((count, 4 * width), BF),
            jax.ShapeDtypeStruct((width, weights.shape[1] // 2), BF),
            jax.ShapeDtypeStruct((width, weights.shape[1] // 2), BF),
        ),
        in_specs=[SMEM_SPEC] + [VMEM_SPEC] * 4,
        out_specs=(VMEM_SPEC,) * 3,
        scratch_shapes=[
            pltpu.VMEM((count, 128), jnp.int32),
            pltpu.VMEM((width, count), BF),
            pltpu.VMEM((count, width), F32),
            pltpu.VMEM((count, width), BF),
            pltpu.VMEM((count, width), BF),
            pltpu.VMEM((count, width), BF),
            pltpu.VMEM((count, width), F32),
            pltpu.VMEM((width, count), BF),
            pltpu.VMEM((count, width), BF),
            pltpu.VMEM((pairs, 2 * TILE, kept), BF),
            pltpu.VMEM((pairs, 2 * TILE, kept), BF),
            pltpu.VMEM((128, count), F32),
            pltpu.VMEM((128, count), F32),
        ],
        compiler_params=pltpu.CompilerParams(vmem_limit_bytes=37 << 20),
        cost_estimate=pl.CostEstimate(
            flops=30_000_000_000, bytes_accessed=12_000_000, transcendentals=10_000_000
        ),
    )(lens, dest, inbox, weights, upstream)


def shards(events, home_slot, dest_slot, seq_lens, weights, out_grad, momentum_in, momentum_out):
    row_count, model_width = events.shape
    home = home_slot.reshape(1, row_count)
    dest = dest_slot.reshape(1, row_count)
    peers = lax.axis_size(DP)
    slots = row_count // peers

    def exchange(blocks):
        return lax.all_to_all(blocks, DP, split_axis=0, concat_axis=0, tiled=True)

    outbox = place(home, events).reshape(peers, slots, model_width)
    inbox = exchange(outbox).reshape(row_count, model_width)
    hidden_grad, kept, given = layer(seq_lens, dest, inbox, weights, out_grad)
    got = lax.ppermute(given, CORE, [(0, 1), (1, 0)])
    sendback = back(dest, hidden_grad, weights, out_grad)
    wire = pack(sendback.reshape(peers, slots, model_width), kept, got)
    grad_scale = (peers * row_count) ** (-0.5)
    return finish(grad_scale, home, exchange(wire), momentum_in, momentum_out)


def solution(mesh):
    split = Mesh(mesh.devices.reshape(4, 4, 4, 2), DP)
    return jax.shard_map(
        shards,
        mesh=split,
        in_specs=(P(DP, None), P(DP), P(DP), P(DP), P(), P(DP, None), P(DP, None), P(DP, None)),
        out_specs=(P(DP, None), P(DP, None), P(DP, None)),
        check_vma=False,
    )
```
